128 devices in a mesh: gz: 4 (over x), gx: 32 (over y, z, core).
Axes of the slice: x: 4, y: 4, z: 4, core: 2. Of those that a mesh axis runs over, the one named last changes fastest.
Arguments:
- populations: float32 [27, 8, 256, 128], P(None, 'gz', 'gx'), may hold values from 0 to 1, as said below
- rates: float32 [27], replicated, may hold values from 0.5 to 1.8
- grain_fraction: bfloat16 [65536, 128], P(('gz', 'gx')), may hold values from 0 to 0.3984375
- grain_velocity: bfloat16 [3, 65536], P(None, ('gz', 'gx')), may hold values from -0.29882812 to 0.29882812
- grain_dest: int32 [65536, 1], P(('gz', 'gx')), may hold values from 0 to 127; in each aligned block of 512 rows (0 to 511, 512 to 1023, ...) at most 8 rows name the same one
- grain_line: int32 [65536], P(('gz', 'gx')), may hold values from 0 to 15
Outputs:
- scaled: float32 [27, 8, 256, 128], P(None, 'gz', 'gx')
- grain_force: float32 [3, 65536], P(None, ('gz', 'gx'))
The draws below stay inside these ranges and needn't reach their ends.
Inputs may be any that keep to these rules, and one draw needn't show every extreme that they name: populations are positive. grain_dest is a linear index of gz+gx, gz slowest; among the rows of one device at most 8 name the same device, and exactly 8 do in some device's rows.
All inputs are finite; a program needn't handle non-finite values.
Results may differ from the reference program's by a relative error of at most 0.0003.
Values may be sent and summed in bfloat16 or wider, within the bound.
A program may use at most 64 MiB of HBM per device.

```python
import math
import jax
import jax.numpy as jnp
import numpy as np
from jax import lax

CZ = 2
CX = 8
NY = 128
G_DEV = 512
STEPS = 2
NZ = 8
NX = 256
GRAINS = 65536
CAP = 8
N_GX = 32
DEVICES = 128


def lattice_columns():
    labels = np.arange(27)
    comp_z = (labels // 9 - 1).astype(np.float32)
    comp_x = (labels // 3 % 3 - 1).astype(np.float32)
    comp_y = (labels % 3 - 1).astype(np.float32)
    count = np.abs(labels // 9 - 1) + np.abs(labels // 3 % 3 - 1) + np.abs(labels % 3 - 1)
    weights = np.array([8.0 / 27, 2.0 / 27, 1.0 / 54, 1.0 / 216], dtype=np.float32)[count]
    return (comp_z, comp_x, comp_y, weights)


def draw_populations(key, part):
    key_density, key_speed, key_noise = jax.random.split(jax.random.fold_in(key, 11), 3)
    comp_z, comp_x, comp_y, weights = lattice_columns()
    grid = (NZ, NX, NY)
    density = 1.0 + jnp.clip(0.03 * jax.random.normal(key_density, grid, jnp.float32), -0.1, 0.1)
    speed = jnp.clip(0.06 * jax.random.normal(key_speed, (3,) + grid, jnp.float32), -0.15, 0.15)
    noise = jax.random.uniform(key_noise, (27,) + grid, jnp.float32, -0.2, 0.2)
    along = jnp.asarray(comp_z)[:, None, None, None] * speed[0][None] + jnp.asarray(comp_x)[:, None, None, None] * speed[1][None] + jnp.asarray(comp_y)[:, None, None, None] * speed[2][None]
    square = jnp.sum(speed * speed, axis=0)
    equil = jnp.asarray(weights)[:, None, None, None] * density[None] * (1.0 + 3.0 * along + 4.5 * along * along - 1.5 * square[None])
    return equil * (1.0 + noise)


def set_ends(values, key, low, largest):
    longest = values.shape.index(max(values.shape))
    spots = []
    for shift in (0, 1):
        where = [jax.random.randint(jax.random.fold_in(key, axis), (), 0, length) for axis, length in enumerate(values.shape)]
        where[longest] = (where[longest] + shift) % values.shape[longest]
        spots.append(tuple(where))
    return values.at[spots[0]].set(low).at[spots[1]].set(largest)


def levels(stream_key, shape, cuts, least, top_value):
    def one(dim, parts):
        heights = jax.random.uniform(jax.random.fold_in(jax.random.fold_in(stream_key, 6), dim), (parts,), jnp.float32, least / len(cuts), top_value / len(cuts))
        return jnp.repeat(jnp.exp(heights), shape[dim] // parts).reshape((-1,) + (1,) * (len(shape) - dim - 1))

    level = one(*cuts[0])
    for cut in cuts[1:]:
        level = level * one(*cut)
    return level


def assign_block(stream_key, own, number, rows, number_of, top, bound, skew):
    sequence = jax.random.permutation(stream_key, number_of)
    crowded, common = load_shares(number_of, rows * top, bound, skew, True), load_shares(number_of, rows * top, bound, skew, False)
    places = jnp.arange(number_of)

    def named(lengths, rotation):
        used = int((lengths > 0).sum())
        fixed = max(1, used // 4)
        shifted = fixed + (places - fixed + rotation * (used - fixed)) % max(1, number_of - fixed)
        return jnp.zeros((number_of,), jnp.int32).at[sequence[jnp.where(places < fixed, places, shifted)]].set(jnp.asarray(lengths, jnp.int32))

    lengths = jnp.where(number % 4 == 0, named(crowded, number // 4), named(common, number - number // 4 - 1))
    mixed = jax.random.permutation(jax.random.fold_in(own, 3), number_of)
    source_of, receiver = mixed[0:number_of // 2 * 2:2], mixed[1:number_of // 2 * 2:2]
    room = jnp.minimum(lengths[source_of] - 1, bound - lengths[receiver]) // 2
    room = jnp.where((source_of == sequence[0]) | (receiver == sequence[0]) | (lengths[receiver] == 0), 0, jnp.maximum(room, 0))
    shifted = jax.random.randint(jax.random.fold_in(own, 4), (number_of // 2,), 0, 1 << 20) % (room + 1)
    lengths = lengths.at[source_of].add(-shifted).at[receiver].add(shifted)
    members = jnp.searchsorted(jnp.cumsum(lengths), jnp.arange(rows * top), side="right").astype(jnp.int32)
    listing = members.reshape(top, rows).T
    listing = listing[jax.random.permutation(jax.random.fold_in(own, 1), rows)]
    rotation = jax.random.randint(jax.random.fold_in(own, 2), (rows, 1), 0, top)
    return jnp.take_along_axis(listing, (jnp.arange(top)[None, :] + rotation) % top, axis=1)


def load_shares(number_of, total, bound, skew, full):
    portions = [(1 << 20) // math.isqrt(standing ** skew) + 1 for standing in range(1, number_of + 1)]
    largest = bound if full else min(bound, max(-(-total // number_of), total * portions[0] // sum(portions)))
    least = 1 if total - largest >= number_of - 1 else 0
    given, surplus = [largest] + [least] * (number_of - 1), total - largest - least * (number_of - 1)
    while surplus > 0:
        free = [i for i in range(1, number_of) if given[i] < largest] or [i for i in range(1, number_of) if given[i] < bound]
        pool, budget = sum([portions[i] for i in free]), surplus
        for i in free:
            addition = min(bound - given[i], max(1, budget * portions[i] // pool), surplus)
            given[i] = given[i] + addition
            surplus = surplus - addition
    return np.array(given)


def gaussian(rng, shape, scale, bound, shards=(), kind=jnp.bfloat16):
    values = jax.random.normal(rng, shape, jnp.float32) * scale
    if len(shards) > 0:
        values = levels(rng, shape, shards, -0.22, 0.18) * values
    return jnp.clip(values, min=-bound, max=bound).astype(kind)


def setup_inputs(seed: int = 0) -> dict:
    key_of = jax.random.split(jax.random.key(seed), 7)
    populations = draw_populations(jax.random.fold_in(key_of[6], 71), 0)
    rates = jnp.clip(jnp.exp(jax.random.uniform(key_of[1], (27,), jnp.float32, math.log(0.5), math.log(1.8))), 0.5, 1.8)
    grain_fraction = jnp.clip(0.3984375 * jax.random.uniform(key_of[2], (GRAINS, NY), jnp.float32) ** levels(key_of[2], (GRAINS, NY), ((0, 128),), -0.2, 0.2), 0.0, 0.3984375).astype(jnp.bfloat16)
    grain_velocity = gaussian(key_of[3], (3, GRAINS), 0.1, 0.29882812, ((1, 128),))
    grain_dest_keys = jax.random.split(jax.random.fold_in(key_of[4], 1), GRAINS // G_DEV)
    grain_dest_turns = jax.random.permutation(jax.random.fold_in(key_of[4], 3), GRAINS // G_DEV)
    grain_dest = jax.vmap(lambda own, number: assign_block(jax.random.fold_in(key_of[4], 2), own, number, G_DEV, DEVICES, 1, CAP, 2))(grain_dest_keys, grain_dest_turns).reshape((GRAINS, 1))
    grain_line = set_ends(jax.random.randint(key_of[5], (GRAINS,), 0, CZ * CX), jax.random.fold_in(key_of[5], 1), 0, (CZ * CX) - 1).astype(jnp.int32)
    return {"populations": populations, "rates": rates, "grain_fraction": grain_fraction, "grain_velocity": grain_velocity, "grain_dest": grain_dest, "grain_line": grain_line}


highest = lax.Precision.HIGHEST


def lattice_tables():
    labels = np.arange(27)
    digits = [labels // 9, (labels // 3) % 3, labels % 3]
    velocity = np.stack([digit - 1 for digit in digits]).astype(np.float32)
    count = np.abs(digits[0] - 1) + np.abs(digits[1] - 1) + np.abs(digits[2] - 1)
    weights = np.array([8.0 / 27, 2.0 / 27, 1.0 / 54, 1.0 / 216], dtype=np.float32)[count]
    vander = np.array([[1.0, 1.0, 1.0], [-1.0, 0.0, 1.0], [1.0, 0.0, 1.0]], dtype=np.float32)
    vander_inv = np.array([[0.0, -0.5, 0.5], [1.0, 0.0, -1.0], [0.0, 0.5, 0.5]], dtype=np.float32)
    moments = np.ones((27, 27), dtype=np.float32)
    inverse = np.ones((27, 27), dtype=np.float32)
    for digit in digits:
        moments = moments * vander[digit[:, None], digit[None, :]]
        inverse = inverse * vander_inv[digit[:, None], digit[None, :]]
    return velocity, weights, moments, inverse


def equilibrium(density, speed, velocity, weights):
    along = jnp.dot(velocity.T, speed, precision=highest)
    square = jnp.sum(speed * speed, axis=0)
    return weights[:, None] * density[None, :] * (1.0 + 3.0 * along + 4.5 * along * along - 1.5 * square[None, :])


def collide(fields, rates, solid, carried):
    velocity_np, weights_np, moments_np, inverse_np = lattice_tables()
    velocity = jnp.asarray(velocity_np)
    weights = jnp.asarray(weights_np)
    density = jnp.sum(fields, axis=0)
    momentum = jnp.dot(velocity, fields, precision=highest)
    speed = momentum / density[None, :]
    equil = equilibrium(density, speed, velocity, weights)
    departure = fields - equil
    projected = jnp.dot(jnp.asarray(moments_np), departure, precision=highest)
    fluid = -jnp.dot(jnp.asarray(inverse_np), rates[:, None] * projected, precision=highest)
    cover = 1.0 + solid
    share = solid / cover
    solid_equil = equilibrium(density, carried / cover[None, :], velocity, weights)
    exchange_term = departure[::-1] - (fields - solid_equil)
    post = fields + (1.0 - share)[None, :] * fluid + share[None, :] * exchange_term
    push = jnp.dot(velocity, exchange_term, precision=highest) / cover[None, :]
    return post, push


def stream(post):
    depth = post.shape[1]
    rows = jnp.arange(depth)[:, None, None]
    moved_list = []
    for population in range(27):
        step_z = population // 9 - 1
        step_x = (population // 3) % 3 - 1
        step_y = population % 3 - 1
        moved = jnp.roll(post[population], (step_z, step_x, step_y), axis=(0, 1, 2))
        if step_z == 1:
            moved = jnp.where(rows == 0, post[26 - population], moved)
        if step_z == -1:
            moved = jnp.where(rows == depth - 1, post[26 - population], moved)
        moved_list.append(moved)
    return jnp.stack(moved_list)


def reference(populations, rates, grain_fraction, grain_velocity, grain_dest, grain_line):
    depth, length, width = populations.shape[1], populations.shape[2], populations.shape[3]
    target = grain_dest[:, 0]
    row_z = (target // N_GX) * CZ + grain_line // CX
    row_x = (target % N_GX) * CX + grain_line % CX
    line_id = (row_z * length + row_x).astype(jnp.int32)
    fraction = grain_fraction.astype(jnp.float32)
    speed = grain_velocity.astype(jnp.float32)
    solid = jax.ops.segment_sum(fraction, line_id, depth * length)
    carried = jnp.stack([jax.ops.segment_sum(fraction * speed[component][:, None], line_id, depth * length) for component in range(3)])
    solid_planes = solid.reshape(depth, length * width)
    carried_planes = jnp.moveaxis(carried.reshape(3, depth, length * width), 1, 0)
    fields = populations
    push_total = jnp.zeros((3, depth, length * width), jnp.float32)

    def collide_plane(items):
        plane, solid_plane, carried_plane = items
        return collide(plane, rates, solid_plane, carried_plane)

    for turn_index in range(STEPS):
        planes = jnp.moveaxis(fields.reshape(27, depth, length * width), 1, 0)
        post, push = lax.map(collide_plane, (planes, solid_planes, carried_planes))
        post = jnp.moveaxis(post, 0, 1).reshape(27, depth, length, width)
        push_total = push_total + jnp.moveaxis(push, 0, 1)
        fields = stream(post)
    weights = jnp.asarray(lattice_tables()[1])
    scaled = fields / weights[:, None, None, None]
    push_lines = push_total.reshape(3, depth * length, width)
    picked = push_lines[:, line_id, :]
    grain_force = -jnp.sum(picked * fraction[None, :, :], axis=2)
    return scaled, grain_force
```

```python
import functools
import itertools

import jax
import jax.numpy as jnp
import numpy as np
from jax import lax
from jax.experimental import pallas as pl
from jax.experimental.pallas import tpu as pltpu
from jax.sharding import PartitionSpec as P

MESH = pl.DeviceIdType.MESH
F32 = jnp.float32
BF16 = jnp.bfloat16
DEV = 128
CAP = 8
GRAINS = 512
SLOTS = DEV * CAP
VEL = [(i // 9 - 1, i // 3 % 3 - 1, i % 3 - 1) for i in range(27)]
WEIGHT = [(8.0 / 27, 2.0 / 27, 1.0 / 54, 1.0 / 216)[sum(map(abs, c))] for c in VEL]
NT = (((1,), (1,)), ((), ()))


def ring(v):
    return min(v, 4 - v)


OFFSETS = sorted(
    (o for o in itertools.product(range(4), range(4), range(4), range(2)) if any(o)),
    key=lambda o: -(ring(o[0]) + ring(o[1]) + ring(o[2]) + 0.3 * o[3]),
)


def iota(shape, dim, dtype=jnp.int32):
    out = lax.broadcasted_iota(jnp.int32, shape, dim)
    return out if dtype == jnp.int32 else out.astype(dtype)


def one_hot(mask):
    return jnp.where(mask, 1.0, 0.0).astype(BF16)


def split(x):
    high = x.astype(BF16)
    low = (x - high.astype(F32)).astype(BF16)
    return high, low


def nt(a, b):
    return lax.dot_general(a, b, NT, preferred_element_type=F32)


def nn(a, b):
    return jnp.dot(a, b, preferred_element_type=F32)


def along_axes(values, triple):
    for stride in (1, 3, 9):
        out = [None] * 27
        for base in range(27):
            if base // stride % 3 == 0:
                idx = (base, base + stride, base + 2 * stride)
                for k, v in zip(idx, triple(*(values[j] for j in idx))):
                    out[k] = v
        values = out
    return values


def to_moments(a, b, c):
    s = a + c
    return s + b, c - a, s


def from_moments(m0, m1, m2):
    h0, h1 = 0.5 * m2, 0.5 * m1
    return h0 - h1, m0 - m2, h0 + h1


def moments(f):
    plane = {}
    rho = None
    mom = [None, None, None]
    for i in range(27):
        rho = f[i] if rho is None else rho + f[i]
        for k in range(3):
            if VEL[i][k]:
                key = (k, VEL[i][k])
                plane[key] = f[i] if key not in plane else plane[key] + f[i]
    for k in range(3):
        mom[k] = plane[(k, 1)] - plane[(k, -1)]
    return rho, mom


def equilibrium(rho, v):
    t = [3.0 * q for q in v]
    base = rho * (1.0 - 1.5 * (v[0] * v[0] + v[1] * v[1] + v[2] * v[2]))
    half = 0.5 * rho
    out = [None] * 27
    for i in range(13):
        along = None
        c = VEL[26 - i]
        for k in range(3):
            if c[k]:
                term = t[k]
                if along is None:
                    along = term if c[k] > 0 else -term
                else:
                    along = along + term if c[k] > 0 else along - term
        even = base + half * (along * along)
        odd = rho * along
        out[26 - i] = WEIGHT[i] * (even + odd)
        out[i] = WEIGHT[i] * (even - odd)
    out[13] = WEIGHT[13] * base
    return out


def kernel(
    pop_in, rates, frac_in, vel_in, dest_in, line_in,
    f_out, force_out,
    pop, frac, vel, dest, line,
    send_f, send_m, recv_f, recv_m, send_r, recv_r,
    keep, mix, post, edge_s, corner_s, edge_r, corner_r, z_r,
    chosen_s, rank_s, match_s, cells,
    in_sem, a_send, a_recv, h_send, h_recv, own_sem,
):
    gz, gx = lax.axis_index("gz"), lax.axis_index("gx")
    me = gz * 32 + gx
    yy, zz, core = gx // 8, gx // 2 % 4, gx % 2

    def peer(o):
        x = lax.rem(gz + o[0], 4)
        rest = lax.rem(yy + o[1], 4) * 8 + lax.rem(zz + o[2], 4) * 2 + lax.rem(core + o[3], 2)
        return x, rest

    barrier = pltpu.get_barrier_semaphore()
    for o in OFFSETS:
        pl.semaphore_signal(barrier, inc=1, device_id=peer(o), device_id_type=MESH)

    loads = [
        pltpu.make_async_copy(src, dst, in_sem.at[k])
        for k, (src, dst) in enumerate(
            ((dest_in, dest), (line_in, line), (vel_in, vel), (frac_in, frac), (pop_in, pop))
        )
    ]
    for load in loads:
        load.start()

    earlier = one_hot(iota((GRAINS, GRAINS), 0) < iota((GRAINS, GRAINS), 1))
    loads[0].wait()
    target = dest[...]
    chosen = iota((DEV, GRAINS), 0) == target
    chosen_b = one_hot(chosen)
    chosen_s[...] = chosen_b
    before = nn(chosen_b, earlier)
    rank = jnp.sum(jnp.where(chosen, before, 0.0), axis=0, keepdims=True)
    rank_mask = jnp.where(iota((CAP, GRAINS), 0, F32) == rank, 1.0, 0.0)
    rank_s[...] = rank_mask

    loads[1].wait()
    loads[2].wait()
    speed = vel[...].astype(F32)
    values = [line[...].astype(F32)] + [speed[k : k + 1] for k in range(3)]
    rows = [rank_mask * v for v in values] + [jnp.zeros((DEV - 4 * CAP, GRAINS), F32)]
    send_m[...] = nt(chosen_b, jnp.concatenate(rows, axis=0).astype(BF16)).reshape(DEV, 1, 128)

    loads[3].wait()
    place = target.astype(F32) * CAP + rank
    fractions = frac[...]
    for j in range(8):
        pick = one_hot(iota((128, GRAINS), 0, F32) + 128.0 * j == place)
        send_f[16 * j : 16 * j + 16] = nn(pick, fractions).astype(BF16).reshape(16, CAP, 128)

    pl.semaphore_wait(barrier, DEV - 1)

    def to_all(src, dst, k):
        for o in OFFSETS:
            d = peer(o)
            pltpu.make_async_remote_copy(
                src_ref=src.at[d[0] * 32 + d[1]],
                dst_ref=dst.at[me],
                send_sem=a_send.at[k],
                recv_sem=a_recv.at[k],
                device_id=d,
                device_id_type=MESH,
            ).start()

    def wait_all(src, dst, sem):
        pltpu.make_async_copy(src.at[pl.ds(0, DEV - 1)], dst.at[pl.ds(0, DEV - 1)], sem).wait()

    to_all(send_m, recv_m, 0)
    to_all(send_f, recv_f, 1)
    own = [
        pltpu.make_async_copy(send_m.at[me], recv_m.at[me], own_sem.at[0]),
        pltpu.make_async_copy(send_f.at[me], recv_f.at[me], own_sem.at[1]),
    ]
    for copy in own:
        copy.start()

    def relax(f, departure, level):
        projected = along_axes(departure, to_moments)
        scaled = [projected[a] * (-rates[a]) for a in range(27)]
        return along_axes(scaled, from_moments)

    def collide(f, rho, mom, level):
        inverse = 1.0 / rho
        equil = equilibrium(rho, [m * inverse for m in mom])
        departure = [f[i] - equil[i] for i in range(27)]
        fluid = relax(f, departure, level)
        for i in range(27):
            keep[i, level] = f[i] + fluid[i]
            mix[i, level] = departure[26 - i] - f[i] - fluid[i]

    def finish(step, level, rho, share, us):
        equil = equilibrium(rho, us)
        for i in range(27):
            post[step, i, level] = keep[i, level] + share * (mix[i, level] + equil[i])

    loads[4].wait()
    first = []
    for level in range(2):
        f = [pop[i, level] for i in range(27)]
        rho, mom = moments(f)
        first.append((rho, mom))
        collide(f, rho, mom, level)

    wait_all(send_m, recv_m, a_recv.at[0])
    own[0].wait()
    diag = iota((CAP, 128), 0) == iota((CAP, 128), 1) % CAP
    spread = jnp.concatenate(
        [jnp.where(diag, jnp.broadcast_to(recv_m[s], (CAP, 128)), 0.0) for s in range(DEV)], axis=0
    ).astype(BF16)
    sel = one_hot(iota((CAP, 128), 0) == iota((CAP, 128), 1) // CAP)
    info = nt(sel, spread)
    match = jnp.where(iota((16, SLOTS), 0, F32) == info[0:1], 1.0, 0.0)
    match_s[...] = match
    weights = jnp.concatenate(
        [match] + [match * info[k : k + 1] for k in range(1, 4)], axis=0
    ).astype(BF16)

    wait_all(send_f, recv_f, a_recv.at[1])
    own[1].wait()
    summed = nn(weights, recv_f[...].reshape(SLOTS, 128))
    covers = []
    for level in range(2):
        at = lambda k: summed[16 * k + 8 * level : 16 * k + 8 * level + 8]
        solid = at(0)
        inverse = 1.0 / (1.0 + solid)
        covers.append((inverse, solid * inverse, [at(k) * inverse for k in range(1, 4)]))

    up, down = gz < 3, gz > 0
    right, left = lax.rem(gx + 1, 32), lax.rem(gx + 31, 32)

    def halo(step):
        def copy(k, src, dst, device):
            return pltpu.make_async_remote_copy(
                src_ref=src,
                dst_ref=dst,
                send_sem=h_send.at[step, k],
                recv_sem=h_recv.at[step, k],
                device_id=device,
                device_id_type=MESH,
            )

        both = [
            copy(0, edge_s.at[step, 0], edge_r.at[step, 0], (gz, right)),
            copy(1, edge_s.at[step, 1], edge_r.at[step, 1], (gz, left)),
        ]
        upward = [
            copy(2, corner_s.at[step, 0, 0], corner_r.at[step, 0, 0], (gz + 1, right)),
            copy(3, corner_s.at[step, 1, 0], corner_r.at[step, 1, 0], (gz + 1, left)),
            copy(4, post.at[step, pl.ds(18, 9), 1], z_r.at[step, 0], (gz + 1, gx)),
        ]
        downward = [
            copy(5, corner_s.at[step, 0, 1], corner_r.at[step, 0, 1], (gz - 1, right)),
            copy(6, corner_s.at[step, 1, 1], corner_r.at[step, 1, 1], (gz - 1, left)),
            copy(7, post.at[step, pl.ds(0, 9), 0], z_r.at[step, 1], (gz - 1, gx)),
        ]
        return both, upward, downward

    def edge_row(i, level):
        cz, _, cy = VEL[i]
        if cz == 0:
            return 3 * level + cy + 1
        return (6 if cz > 0 else 9) + cy + 1

    def is_corner(i, level):
        return (VEL[i][0] > 0 and level == 1) or (VEL[i][0] < 0 and level == 0)

    def send_halo(step):
        for i in range(27):
            cz, cx, cy = VEL[i]
            if cx == 0:
                continue
            side, row = (0, 7) if cx > 0 else (1, 0)
            for level in range(2):
                edge = post[step, i, level, row : row + 1, :]
                if is_corner(i, level):
                    corner_s[step, side, 0 if cz > 0 else 1, cy + 1 : cy + 2, :] = edge
                else:
                    k = edge_row(i, level)
                    edge_s[step, side, k : k + 1, :] = edge
        both, upward, downward = halo(step)

        @pl.when(up)
        def _():
            for c in upward:
                c.start()

        @pl.when(down)
        def _():
            for c in downward:
                c.start()

        for c in both:
            c.start()

    def wait_halo(step):
        both, upward, downward = halo(step)
        for c in both:
            c.wait_recv()

        @pl.when(down)
        def _():
            for c in upward:
                c.wait_recv()

        @pl.when(up)
        def _():
            for c in downward:
                c.wait_recv()

    sub = iota((8, 128), 0)

    def streamed(step, i, level):
        cz, cx, cy = VEL[i]
        origin = level - cz
        outside = origin < 0 or origin > 1
        if outside:
            z_side = 0 if cz > 0 else 1
            value = z_r[step, z_side, i - 18 if cz > 0 else i]
        else:
            value = post[step, i, origin]
        if cx:
            side = 0 if cx > 0 else 1
            if outside:
                row = corner_r[step, side, z_side, cy + 1 : cy + 2, :]
            else:
                k = edge_row(i, origin)
                row = edge_r[step, side, k : k + 1, :]
            value = pltpu.roll(value, cx % 8, 0)
            value = jnp.where(sub == (0 if cx > 0 else 7), jnp.broadcast_to(row, (8, 128)), value)
        if cy:
            value = pltpu.roll(value, cy % 128, 1)
        if outside:
            wall = gz == 0 if cz > 0 else gz == 3
            value = jnp.where(wall, post[step, 26 - i, level], value)
        return value

    for level in range(2):
        _, share, us = covers[level]
        finish(0, level, first[level][0], share, us)
    send_halo(0)
    wait_halo(0)

    second = []
    pushes = [[None, None] for _ in range(3)]
    for level in range(2):
        f = []
        for i in range(27):
            v = streamed(0, i, level)
            cells[i, level] = v
            f.append(v)
        rho, mom = moments(f)
        second.append((rho, mom))
        inverse, _, us = covers[level]
        rho_sum = first[level][0] + rho
        for k in range(3):
            pushes[k][level] = (us[k] * rho_sum - (first[level][1][k] + mom[k])) * inverse

    push = jnp.concatenate([pushes[k][level] for k in range(3) for level in range(2)], axis=0)
    high, low = split(-push)
    grains = recv_f[...].reshape(SLOTS, 128)
    all_lines = nt(high, grains) + nt(low, grains)
    match = match_s[...]
    diag = iota((CAP, SLOTS), 0) == iota((CAP, SLOTS), 1) % CAP
    parts = []
    for k in range(3):
        force = jnp.sum(match * all_lines[16 * k : 16 * k + 16], axis=0, keepdims=True)
        parts.append(jnp.where(diag, force, 0.0))
    parts.append(jnp.zeros((DEV - 3 * CAP, SLOTS), F32))
    high, low = split(jnp.concatenate(parts, axis=0))
    owner = one_hot(iota((DEV, SLOTS), 0) == iota((DEV, SLOTS), 1) // CAP)
    send_r[...] = (nt(owner, high) + nt(owner, low)).reshape(DEV, 1, 128)
    to_all(send_r, recv_r, 2)
    own_r = pltpu.make_async_copy(send_r.at[me], recv_r.at[me], own_sem.at[2])
    own_r.start()

    for level in range(2):
        f = [cells[i, level] for i in range(27)]
        rho, mom = second[level]
        collide(f, rho, mom, level)
        _, share, us = covers[level]
        finish(1, level, rho, share, us)
    send_halo(1)
    wait_halo(1)
    for level in range(2):
        for i in range(27):
            f_out[i, level] = streamed(1, i, level)

    wait_all(send_r, recv_r, a_recv.at[2])
    own_r.wait()
    table = recv_r[...].reshape(DEV, 128).T[0 : 3 * CAP]
    high, low = split(table)
    chosen_b = chosen_s[...]
    per_grain = nn(high, chosen_b) + nn(low, chosen_b)
    rank_mask = rank_s[...]
    for k in range(3):
        force_out[k : k + 1, :] = jnp.sum(
            rank_mask * per_grain[CAP * k : CAP * k + CAP], axis=0, keepdims=True
        )

    wait_all(send_m, recv_m, a_send.at[0])
    wait_all(send_f, recv_f, a_send.at[1])
    wait_all(send_r, recv_r, a_send.at[2])
    for step in range(2):
        both, upward, downward = halo(step)
        for c in both:
            c.wait_send()

        @pl.when(up)
        def _():
            for c in upward:
                c.wait_send()

        @pl.when(down)
        def _():
            for c in downward:
                c.wait_send()


def per_device(populations, rates, grain_fraction, grain_velocity, grain_dest, grain_line):
    hbm = pl.BlockSpec(memory_space=pl.ANY)
    vmem = pl.BlockSpec(memory_space=pltpu.VMEM)
    dma = pltpu.SemaphoreType.DMA
    block = (27, 2, 8, 128)
    cells, force = pl.pallas_call(
        kernel,
        out_shape=(
            jax.ShapeDtypeStruct(block, F32),
            jax.ShapeDtypeStruct((3, GRAINS), F32),
        ),
        in_specs=[hbm, pl.BlockSpec(memory_space=pltpu.SMEM), hbm, hbm, hbm, hbm],
        out_specs=(vmem, vmem),
        scratch_shapes=[
            pltpu.VMEM(block, F32),
            pltpu.VMEM((GRAINS, 128), BF16),
            pltpu.VMEM((3, GRAINS), BF16),
            pltpu.VMEM((1, GRAINS), jnp.int32),
            pltpu.VMEM((1, GRAINS), jnp.int32),
            pltpu.VMEM((DEV, CAP, 128), BF16),
            pltpu.VMEM((DEV, 1, 128), F32),
            pltpu.VMEM((DEV, CAP, 128), BF16),
            pltpu.VMEM((DEV, 1, 128), F32),
            pltpu.VMEM((DEV, 1, 128), F32),
            pltpu.VMEM((DEV, 1, 128), F32),
            pltpu.VMEM(block, F32),
            pltpu.VMEM(block, F32),
            pltpu.VMEM((2,) + block, F32),
            pltpu.VMEM((2, 2, 16, 128), F32),
            pltpu.VMEM((2, 2, 2, 8, 128), F32),
            pltpu.VMEM((2, 2, 16, 128), F32),
            pltpu.VMEM((2, 2, 2, 8, 128), F32),
            pltpu.VMEM((2, 2, 9, 8, 128), F32),
            pltpu.VMEM((DEV, GRAINS), BF16),
            pltpu.VMEM((CAP, GRAINS), F32),
            pltpu.VMEM((16, SLOTS), F32),
            pltpu.VMEM(block, F32),
            dma((5,)),
            dma((3,)),
            dma((3,)),
            dma((2, 8)),
            dma((2, 8)),
            dma((3,)),
        ],
        compiler_params=pltpu.CompilerParams(collective_id=0, has_side_effects=True),
        name="lattice",
    )(
        populations,
        rates,
        grain_fraction,
        grain_velocity,
        grain_dest.reshape(1, GRAINS),
        grain_line.reshape(1, GRAINS),
    )
    scale = np.array([1.0 / w for w in WEIGHT], np.float32)[:, None, None, None]
    return cells * jnp.asarray(scale), force


def solution(mesh):
    in_specs = (
        P(None, "gz", "gx", None),
        P(),
        P(("gz", "gx"), None),
        P(None, ("gz", "gx")),
        P(("gz", "gx"), None),
        P(("gz", "gx")),
    )
    out_specs = (P(None, "gz", "gx", None), P(None, ("gz", "gx")))
    return jax.shard_map(
        per_device, mesh=mesh, in_specs=in_specs, out_specs=out_specs, check_vma=False
    )
```

```python
import functools
import itertools

import jax
import jax.numpy as jnp
from jax import lax
from jax.experimental import pallas as pl
from jax.experimental.pallas import tpu as pltpu
from jax.sharding import PartitionSpec as P

MESH = pl.DeviceIdType.MESH
F32 = jnp.float32
BF16 = jnp.bfloat16
DEV = 128
CAP = 8
GRAINS = 512
SLOTS = DEV * CAP
VEL = [(i // 9 - 1, i // 3 % 3 - 1, i % 3 - 1) for i in range(27)]
WEIGHT = [(8.0 / 27, 2.0 / 27, 1.0 / 54, 1.0 / 216)[sum(map(abs, c))] for c in VEL]
NT = (((1,), (1,)), ((), ()))


def ring(v):
    return min(v, 4 - v)


OFFSETS = sorted(
    (o for o in itertools.product(range(4), range(4), range(4), range(2)) if any(o)),
    key=lambda o: -(ring(o[0]) + ring(o[1]) + ring(o[2]) + 0.3 * o[3]),
)


def iota(shape, dim, dtype=jnp.int32):
    out = lax.broadcasted_iota(jnp.int32, shape, dim)
    return out if dtype == jnp.int32 else out.astype(dtype)


def one_hot(mask):
    return jnp.where(mask, 1.0, 0.0).astype(BF16)


def split(x):
    high = x.astype(BF16)
    low = (x - high.astype(F32)).astype(BF16)
    return high, low


def nt(a, b):
    return lax.dot_general(a, b, NT, preferred_element_type=F32)


def nn(a, b):
    return jnp.dot(a, b, preferred_element_type=F32)


def along_axes(values, triple):
    for stride in (1, 3, 9):
        out = [None] * 27
        for base in range(27):
            if base // stride % 3 == 0:
                idx = (base, base + stride, base + 2 * stride)
                for k, v in zip(idx, triple(*(values[j] for j in idx))):
                    out[k] = v
        values = out
    return values


def to_moments(a, b, c):
    s = a + c
    return s + b, c - a, s


def from_moments(m0, m1, m2):
    h0, h1 = 0.5 * m2, 0.5 * m1
    return h0 - h1, m0 - m2, h0 + h1


def moments(f):
    plane = {}
    rho = None
    mom = [None, None, None]
    for i in range(27):
        rho = f[i] if rho is None else rho + f[i]
        for k in range(3):
            if VEL[i][k]:
                key = (k, VEL[i][k])
                plane[key] = f[i] if key not in plane else plane[key] + f[i]
    for k in range(3):
        mom[k] = plane[(k, 1)] - plane[(k, -1)]
    return rho, mom


def equilibrium(rho, v):
    t = [3.0 * q for q in v]
    base = rho * (1.0 - 1.5 * (v[0] * v[0] + v[1] * v[1] + v[2] * v[2]))
    half = 0.5 * rho
    out = [None] * 27
    for i in range(13):
        along = None
        c = VEL[26 - i]
        for k in range(3):
            if c[k]:
                term = t[k]
                if along is None:
                    along = term if c[k] > 0 else -term
                else:
                    along = along + term if c[k] > 0 else along - term
        even = base + half * (along * along)
        odd = rho * along
        out[26 - i] = WEIGHT[i] * (even + odd)
        out[i] = WEIGHT[i] * (even - odd)
    out[13] = WEIGHT[13] * base
    return out


def kernel(
    pop_in, rates_in, frac_in, vel_in, dest_in, line_in,
    f_out, force_out,
    rates, pop, frac, vel, dest, line,
    send_f, send_m, recv_f, recv_m, send_r, recv_r,
    keep, mix, post, edge_s, corner_s, edge_r, corner_r, z_r,
    chosen_s, rank_s, match_s, cells,
    in_sem, a_send, a_recv, h_send, h_recv, own_sem,
):
    gz, gx = lax.axis_index("gz"), lax.axis_index("gx")
    me = gz * 32 + gx
    yy, zz, core = gx // 8, gx // 2 % 4, gx % 2

    def peer(o):
        x = lax.rem(gz + o[0], 4)
        rest = lax.rem(yy + o[1], 4) * 8 + lax.rem(zz + o[2], 4) * 2 + lax.rem(core + o[3], 2)
        return x, rest

    barrier = pltpu.get_barrier_semaphore()
    for o in OFFSETS:
        pl.semaphore_signal(barrier, inc=1, device_id=peer(o), device_id_type=MESH)

    loads = [
        pltpu.make_async_copy(src, dst, in_sem.at[k])
        for k, (src, dst) in enumerate(
            ((dest_in, dest), (line_in, line), (vel_in, vel), (frac_in, frac), (pop_in, pop), (rates_in, rates))
        )
    ]
    for load in loads:
        load.start()

    earlier = one_hot(iota((GRAINS, GRAINS), 0) < iota((GRAINS, GRAINS), 1))
    loads[0].wait()
    target = dest[...]
    chosen = iota((DEV, GRAINS), 0) == target
    chosen_b = one_hot(chosen)
    chosen_s[...] = chosen_b
    before = nn(chosen_b, earlier)
    rank = jnp.sum(jnp.where(chosen, before, 0.0), axis=0, keepdims=True)
    rank_mask = jnp.where(iota((CAP, GRAINS), 0, F32) == rank, 1.0, 0.0)
    rank_s[...] = rank_mask

    loads[1].wait()
    loads[2].wait()
    speed = vel[...].astype(F32)
    values = [line[...].astype(F32)] + [speed[k : k + 1] for k in range(3)]
    rows = [rank_mask * v for v in values] + [jnp.zeros((DEV - 4 * CAP, GRAINS), F32)]
    send_m[...] = nt(chosen_b, jnp.concatenate(rows, axis=0).astype(BF16)).reshape(DEV, 1, 128)

    loads[3].wait()
    place = target.astype(F32) * CAP + rank
    fractions = frac[...]
    for j in range(8):
        pick = one_hot(iota((128, GRAINS), 0, F32) + 128.0 * j == place)
        send_f[16 * j : 16 * j + 16] = nn(pick, fractions).astype(BF16).reshape(16, CAP, 128)

    pl.semaphore_wait(barrier, DEV - 1)

    def to_all(src, dst, k):
        for o in OFFSETS:
            d = peer(o)
            pltpu.make_async_remote_copy(
                src_ref=src.at[d[0] * 32 + d[1]],
                dst_ref=dst.at[me],
                send_sem=a_send.at[k],
                recv_sem=a_recv.at[k],
                device_id=d,
                device_id_type=MESH,
            ).start()

    def wait_all(src, dst, sem):
        pltpu.make_async_copy(src.at[pl.ds(0, DEV - 1)], dst.at[pl.ds(0, DEV - 1)], sem).wait()

    to_all(send_m, recv_m, 0)
    to_all(send_f, recv_f, 1)
    own = [
        pltpu.make_async_copy(send_m.at[me], recv_m.at[me], own_sem.at[0]),
        pltpu.make_async_copy(send_f.at[me], recv_f.at[me], own_sem.at[1]),
    ]
    for copy in own:
        copy.start()

    def relax(f, departure, level):
        projected = along_axes(departure, to_moments)
        scaled = [projected[a] * (-rates[a]) for a in range(27)]
        return along_axes(scaled, from_moments)

    def collide(f, rho, mom, level):
        inverse = 1.0 / rho
        equil = equilibrium(rho, [m * inverse for m in mom])
        departure = [f[i] - equil[i] for i in range(27)]
        fluid = relax(f, departure, level)
        for i in range(27):
            keep[i, level] = f[i] + fluid[i]
            mix[i, level] = departure[26 - i] - f[i] - fluid[i]

    def finish(step, level, rho, share, us):
        equil = equilibrium(rho, us)
        for i in range(27):
            post[step, i, level] = keep[i, level] + share * (mix[i, level] + equil[i])

    loads[4].wait()
    loads[5].wait()
    first = []
    for level in range(2):
        f = [pop[i, level] for i in range(27)]
        rho, mom = moments(f)
        first.append((rho, mom))
        collide(f, rho, mom, level)

    wait_all(send_m, recv_m, a_recv.at[0])
    own[0].wait()
    diag = iota((CAP, 128), 0) == iota((CAP, 128), 1) % CAP
    spread = jnp.concatenate(
        [jnp.where(diag, jnp.broadcast_to(recv_m[s], (CAP, 128)), 0.0) for s in range(DEV)], axis=0
    ).astype(BF16)
    sel = one_hot(iota((CAP, 128), 0) == iota((CAP, 128), 1) // CAP)
    info = nt(sel, spread)
    match = jnp.where(iota((16, SLOTS), 0, F32) == info[0:1], 1.0, 0.0)
    match_s[...] = match
    weights = jnp.concatenate(
        [match] + [match * info[k : k + 1] for k in range(1, 4)], axis=0
    ).astype(BF16)

    wait_all(send_f, recv_f, a_recv.at[1])
    own[1].wait()
    summed = nn(weights, recv_f[...].reshape(SLOTS, 128))
    covers = []
    for level in range(2):
        at = lambda k: summed[16 * k + 8 * level : 16 * k + 8 * level + 8]
        solid = at(0)
        inverse = 1.0 / (1.0 + solid)
        covers.append((inverse, solid * inverse, [at(k) * inverse for k in range(1, 4)]))

    up, down = gz < 3, gz > 0
    right, left = lax.rem(gx + 1, 32), lax.rem(gx + 31, 32)

    def halo(step):
        def copy(k, src, dst, device):
            return pltpu.make_async_remote_copy(
                src_ref=src,
                dst_ref=dst,
                send_sem=h_send.at[step, k],
                recv_sem=h_recv.at[step, k],
                device_id=device,
                device_id_type=MESH,
            )

        both = [
            copy(0, edge_s.at[step, 0], edge_r.at[step, 0], (gz, right)),
            copy(1, edge_s.at[step, 1], edge_r.at[step, 1], (gz, left)),
        ]
        upward = [
            copy(2, corner_s.at[step, 0, 0], corner_r.at[step, 0, 0], (gz + 1, right)),
            copy(3, corner_s.at[step, 1, 0], corner_r.at[step, 1, 0], (gz + 1, left)),
            copy(4, post.at[step, pl.ds(18, 9), 1], z_r.at[step, 0], (gz + 1, gx)),
        ]
        downward = [
            copy(5, corner_s.at[step, 0, 1], corner_r.at[step, 0, 1], (gz - 1, right)),
            copy(6, corner_s.at[step, 1, 1], corner_r.at[step, 1, 1], (gz - 1, left)),
            copy(7, post.at[step, pl.ds(0, 9), 0], z_r.at[step, 1], (gz - 1, gx)),
        ]
        return both, upward, downward

    def edge_row(i, level):
        cz, _, cy = VEL[i]
        if cz == 0:
            return 3 * level + cy + 1
        return (6 if cz > 0 else 9) + cy + 1

    def is_corner(i, level):
        return (VEL[i][0] > 0 and level == 1) or (VEL[i][0] < 0 and level == 0)

    def send_halo(step):
        for i in range(27):
            cz, cx, cy = VEL[i]
            if cx == 0:
                continue
            side, row = (0, 7) if cx > 0 else (1, 0)
            for level in range(2):
                edge = post[step, i, level, row : row + 1, :]
                if is_corner(i, level):
                    corner_s[step, side, 0 if cz > 0 else 1, cy + 1 : cy + 2, :] = edge
                else:
                    k = edge_row(i, level)
                    edge_s[step, side, k : k + 1, :] = edge
        both, upward, downward = halo(step)

        @pl.when(up)
        def _():
            for c in upward:
                c.start()

        @pl.when(down)
        def _():
            for c in downward:
                c.start()

        for c in both:
            c.start()

    def wait_halo(step):
        both, upward, downward = halo(step)
        for c in both:
            c.wait_recv()

        @pl.when(down)
        def _():
            for c in upward:
                c.wait_recv()

        @pl.when(up)
        def _():
            for c in downward:
                c.wait_recv()

    sub = iota((8, 128), 0)

    def streamed(step, i, level):
        cz, cx, cy = VEL[i]
        origin = level - cz
        outside = origin < 0 or origin > 1
        if outside:
            z_side = 0 if cz > 0 else 1
            value = z_r[step, z_side, i - 18 if cz > 0 else i]
        else:
            value = post[step, i, origin]
        if cx:
            side = 0 if cx > 0 else 1
            if outside:
                row = corner_r[step, side, z_side, cy + 1 : cy + 2, :]
            else:
                k = edge_row(i, origin)
                row = edge_r[step, side, k : k + 1, :]
            value = pltpu.roll(value, cx % 8, 0)
            value = jnp.where(sub == (0 if cx > 0 else 7), jnp.broadcast_to(row, (8, 128)), value)
        if cy:
            value = pltpu.roll(value, cy % 128, 1)
        if outside:
            wall = gz == 0 if cz > 0 else gz == 3
            value = jnp.where(wall, post[step, 26 - i, level], value)
        return value

    for level in range(2):
        _, share, us = covers[level]
        finish(0, level, first[level][0], share, us)
    send_halo(0)
    wait_halo(0)

    second = []
    pushes = [[None, None] for _ in range(3)]
    for level in range(2):
        f = []
        for i in range(27):
            v = streamed(0, i, level)
            cells[i, level] = v
            f.append(v)
        rho, mom = moments(f)
        second.append((rho, mom))
        inverse, _, us = covers[level]
        rho_sum = first[level][0] + rho
        for k in range(3):
            pushes[k][level] = (us[k] * rho_sum - (first[level][1][k] + mom[k])) * inverse

    push = jnp.concatenate([pushes[k][level] for k in range(3) for level in range(2)], axis=0)
    high, low = split(-push)
    grains = recv_f[...].reshape(SLOTS, 128)
    all_lines = nt(high, grains) + nt(low, grains)
    match = match_s[...]
    diag = iota((CAP, SLOTS), 0) == iota((CAP, SLOTS), 1) % CAP
    parts = []
    for k in range(3):
        force = jnp.sum(match * all_lines[16 * k : 16 * k + 16], axis=0, keepdims=True)
        parts.append(jnp.where(diag, force, 0.0))
    parts.append(jnp.zeros((DEV - 3 * CAP, SLOTS), F32))
    high, low = split(jnp.concatenate(parts, axis=0))
    owner = one_hot(iota((DEV, SLOTS), 0) == iota((DEV, SLOTS), 1) // CAP)
    send_r[...] = (nt(owner, high) + nt(owner, low)).reshape(DEV, 1, 128)
    to_all(send_r, recv_r, 2)
    own_r = pltpu.make_async_copy(send_r.at[me], recv_r.at[me], own_sem.at[2])
    own_r.start()

    for level in range(2):
        f = [cells[i, level] for i in range(27)]
        rho, mom = second[level]
        collide(f, rho, mom, level)
        _, share, us = covers[level]
        finish(1, level, rho, share, us)
    send_halo(1)
    wait_halo(1)
    for level in range(2):
        for i in range(27):
            f_out[i, level] = streamed(1, i, level) * (1.0 / WEIGHT[i])

    wait_all(send_r, recv_r, a_recv.at[2])
    own_r.wait()
    table = recv_r[...].reshape(DEV, 128).T[0 : 3 * CAP]
    high, low = split(table)
    chosen_b = chosen_s[...]
    per_grain = nn(high, chosen_b) + nn(low, chosen_b)
    rank_mask = rank_s[...]
    for k in range(3):
        force_out[k : k + 1, :] = jnp.sum(
            rank_mask * per_grain[CAP * k : CAP * k + CAP], axis=0, keepdims=True
        )

    wait_all(send_m, recv_m, a_send.at[0])
    wait_all(send_f, recv_f, a_send.at[1])
    wait_all(send_r, recv_r, a_send.at[2])
    for step in range(2):
        both, upward, downward = halo(step)
        for c in both:
            c.wait_send()

        @pl.when(up)
        def _():
            for c in upward:
                c.wait_send()

        @pl.when(down)
        def _():
            for c in downward:
                c.wait_send()


def write_out(cells, force, cells_out, force_out, sem):
    copies = [
        pltpu.make_async_copy(cells, cells_out, sem.at[0]),
        pltpu.make_async_copy(force, force_out, sem.at[1]),
    ]
    for c in copies:
        c.start()
    for c in copies:
        c.wait()


def per_device(populations, rates, grain_fraction, grain_velocity, grain_dest, grain_line):
    hbm = pl.BlockSpec(memory_space=pl.ANY)
    vmem = pl.BlockSpec(memory_space=pltpu.VMEM)
    dma = pltpu.SemaphoreType.DMA
    block = (27, 2, 8, 128)
    cells, force = pl.pallas_call(
        kernel,
        out_shape=(
            pltpu.VMEM(block, F32),
            pltpu.VMEM((3, GRAINS), F32),
        ),
        in_specs=[hbm] * 6,
        out_specs=(vmem, vmem),
        scratch_shapes=[
            pltpu.SMEM((27,), F32),
            pltpu.VMEM(block, F32),
            pltpu.VMEM((GRAINS, 128), BF16),
            pltpu.VMEM((3, GRAINS), BF16),
            pltpu.VMEM((1, GRAINS), jnp.int32),
            pltpu.VMEM((1, GRAINS), jnp.int32),
            pltpu.VMEM((DEV, CAP, 128), BF16),
            pltpu.VMEM((DEV, 1, 128), F32),
            pltpu.VMEM((DEV, CAP, 128), BF16),
            pltpu.VMEM((DEV, 1, 128), F32),
            pltpu.VMEM((DEV, 1, 128), F32),
            pltpu.VMEM((DEV, 1, 128), F32),
            pltpu.VMEM(block, F32),
            pltpu.VMEM(block, F32),
            pltpu.VMEM((2,) + block, F32),
            pltpu.VMEM((2, 2, 16, 128), F32),
            pltpu.VMEM((2, 2, 2, 8, 128), F32),
            pltpu.VMEM((2, 2, 16, 128), F32),
            pltpu.VMEM((2, 2, 2, 8, 128), F32),
            pltpu.VMEM((2, 2, 9, 8, 128), F32),
            pltpu.VMEM((DEV, GRAINS), BF16),
            pltpu.VMEM((CAP, GRAINS), F32),
            pltpu.VMEM((16, SLOTS), F32),
            pltpu.VMEM(block, F32),
            dma((6,)),
            dma((3,)),
            dma((3,)),
            dma((2, 8)),
            dma((2, 8)),
            dma((3,)),
        ],
        compiler_params=pltpu.CompilerParams(collective_id=0, has_side_effects=True),
        name="lattice",
    )(
        populations,
        rates,
        grain_fraction,
        grain_velocity,
        grain_dest.reshape(1, GRAINS),
        grain_line.reshape(1, GRAINS),
    )
    return pl.pallas_call(
        write_out,
        out_shape=(jax.ShapeDtypeStruct(block, F32), jax.ShapeDtypeStruct((3, GRAINS), F32)),
        in_specs=[hbm, hbm],
        out_specs=(hbm, hbm),
        scratch_shapes=[dma((2,))],
        compiler_params=pltpu.CompilerParams(vmem_limit_bytes=1 << 20),
        name="write_out",
    )(cells, force)


def solution(mesh):
    in_specs = (
        P(None, "gz", "gx", None),
        P(),
        P(("gz", "gx"), None),
        P(None, ("gz", "gx")),
        P(("gz", "gx"), None),
        P(("gz", "gx")),
    )
    out_specs = (P(None, "gz", "gx", None), P(None, ("gz", "gx")))
    return jax.shard_map(
        per_device, mesh=mesh, in_specs=in_specs, out_specs=out_specs, check_vma=False
    )
```

```python
import functools
import itertools

import jax
import jax.numpy as jnp
from jax import lax
from jax.experimental import pallas as pl
from jax.experimental.pallas import tpu as pltpu
from jax.sharding import PartitionSpec as P

MESH = pl.DeviceIdType.MESH
F32 = jnp.float32
BF16 = jnp.bfloat16
DEV = 128
CAP = 8
GRAINS = 512
SLOTS = DEV * CAP
VEL = [(i // 9 - 1, i // 3 % 3 - 1, i % 3 - 1) for i in range(27)]
WEIGHT = [(8.0 / 27, 2.0 / 27, 1.0 / 54, 1.0 / 216)[sum(map(abs, c))] for c in VEL]
NT = (((1,), (1,)), ((), ()))


def ring(v):
    return min(v, 4 - v)


OFFSETS = sorted(
    (o for o in itertools.product(range(4), range(4), range(4), range(2)) if any(o)),
    key=lambda o: -(0.75 * (ring(o[0]) + ring(o[1]) + ring(o[2])) + 0.5 * sum(v > 0 for v in o[:3]) + 0.2 * o[3]),
)


def iota(shape, dim, dtype=jnp.int32):
    out = lax.broadcasted_iota(jnp.int32, shape, dim)
    return out if dtype == jnp.int32 else out.astype(dtype)


def one_hot(mask):
    return jnp.where(mask, 1.0, 0.0).astype(BF16)


def split(x):
    high = x.astype(BF16)
    low = (x - high.astype(F32)).astype(BF16)
    return high, low


def nt(a, b):
    return lax.dot_general(a, b, NT, preferred_element_type=F32)


def nn(a, b):
    return jnp.dot(a, b, preferred_element_type=F32)


def along_axes(values, triple):
    for stride in (1, 3, 9):
        out = [None] * 27
        for base in range(27):
            if base // stride % 3 == 0:
                idx = (base, base + stride, base + 2 * stride)
                for k, v in zip(idx, triple(*(values[j] for j in idx))):
                    out[k] = v
        values = out
    return values


def to_moments(a, b, c):
    s = a + c
    return s + b, c - a, s


def from_moments(m0, m1, m2):
    h0, h1 = 0.5 * m2, 0.5 * m1
    return h0 - h1, m0 - m2, h0 + h1


def moments(f):
    plane = {}
    for i in range(27):
        if f[i] is not None:
            for key in [None] + [(k, VEL[i][k]) for k in range(3) if VEL[i][k]]:
                plane[key] = f[i] if key not in plane else plane[key] + f[i]

    def along(k):
        if (k, 1) not in plane:
            return -plane[(k, -1)] if (k, -1) in plane else jnp.zeros_like(plane[None])
        return plane[(k, 1)] - plane[(k, -1)] if (k, -1) in plane else plane[(k, 1)]

    return plane[None], [along(k) for k in range(3)]


def add_moments(a, b):
    return a[0] + b[0], [p + q for p, q in zip(a[1], b[1])]


def equilibrium(rho, v):
    t = [3.0 * q for q in v]
    base = rho * (1.0 - 1.5 * (v[0] * v[0] + v[1] * v[1] + v[2] * v[2]))
    half = 0.5 * rho
    out = [None] * 27
    for i in range(13):
        along = None
        c = VEL[26 - i]
        for k in range(3):
            if c[k]:
                term = t[k]
                if along is None:
                    along = term if c[k] > 0 else -term
                else:
                    along = along + term if c[k] > 0 else along - term
        even = base + half * (along * along)
        odd = rho * along
        out[26 - i] = WEIGHT[i] * (even + odd)
        out[i] = WEIGHT[i] * (even - odd)
    out[13] = WEIGHT[13] * base
    return out


def kernel(
    pop_in, rates_in, frac_in, vel_in, dest_in, line_in,
    f_out, force_out,
    rates, pop, frac, vel, dest, line,
    send_f, send_m, recv_f, recv_m, send_r, recv_r,
    keep, mix, post, edge_s, edge_r, z_s, z_r,
    chosen_s, rank_s, match_s, cells,
    in_sem, a_send, a_recv, h_send, h_recv,
):
    gz, gx = lax.axis_index("gz"), lax.axis_index("gx")
    me = gz * 32 + gx
    yy, zz, core = gx // 8, gx // 2 % 4, gx % 2
    at_x = [lax.rem(gz + a, 4) for a in range(4)]
    at_y = [lax.rem(yy + b, 4) * 8 for b in range(4)]
    at_z = [lax.rem(zz + c, 4) * 2 for c in range(4)]
    at_core = [core, 1 - core]

    def peer(o):
        return at_x[o[0]], at_y[o[1]] + (at_z[o[2]] + at_core[o[3]])

    barrier = pltpu.get_barrier_semaphore()
    for o in OFFSETS:
        pl.semaphore_signal(barrier, inc=1, device_id=peer(o), device_id_type=MESH)

    loads = [
        pltpu.make_async_copy(src, dst, in_sem.at[k])
        for k, (src, dst) in enumerate(
            (
                (dest_in, dest),
                (line_in, line),
                (vel_in, vel),
                (frac_in, frac),
                (pop_in, pop),
                (rates_in, rates),
            )
        )
    ]
    for load in loads:
        load.start()

    earlier = one_hot(iota((GRAINS, GRAINS), 0) < iota((GRAINS, GRAINS), 1))
    loads[0].wait()
    target = dest[...]
    chosen = iota((DEV, GRAINS), 0) == target
    chosen_b = one_hot(chosen)
    chosen_s[...] = chosen_b
    before = nn(chosen_b, earlier)
    rank = jnp.sum(jnp.where(chosen, before, 0.0), axis=0, keepdims=True)
    rank_mask = jnp.where(iota((CAP, GRAINS), 0, F32) == rank, 1.0, 0.0)
    rank_s[...] = rank_mask

    loads[1].wait()
    loads[2].wait()
    speed = vel[...].astype(F32)
    values = [line[...].astype(F32)] + [speed[k : k + 1] for k in range(3)]
    rows = [rank_mask * v for v in values] + [jnp.zeros((DEV - 4 * CAP, GRAINS), F32)]
    send_m[...] = nt(chosen_b, jnp.concatenate(rows, axis=0).astype(BF16))

    loads[3].wait()
    place = target.astype(F32) * CAP + rank
    fractions = frac[...]
    for j in range(8):
        pick = one_hot(iota((128, GRAINS), 0, F32) + 128.0 * j == place)
        send_f[16 * j : 16 * j + 16] = nn(pick, fractions).astype(BF16).reshape(16, CAP, 128)
    recv_m[pl.ds(me, 1), :] = send_m[pl.ds(me, 1), :]
    recv_f[me] = send_f[me]

    pl.semaphore_wait(barrier, DEV - 1)

    def to_peer(o, src, dst, k, wide):
        d = peer(o)
        p = d[0] * 32 + d[1]
        pltpu.make_async_remote_copy(
            src_ref=src.at[p] if wide else src.at[pl.ds(p, 1)],
            dst_ref=dst.at[me] if wide else dst.at[pl.ds(me, 1)],
            send_sem=a_send.at[k],
            recv_sem=a_recv.at[k],
            device_id=d,
            device_id_type=MESH,
        ).start()

    def wait_all(src, dst, sem):
        pltpu.make_async_copy(src.at[pl.ds(0, DEV - 1)], dst.at[pl.ds(0, DEV - 1)], sem).wait()

    for o in OFFSETS:
        to_peer(o, send_m, recv_m, 0, False)
        to_peer(o, send_f, recv_f, 1, True)

    def collide(f, rho, mom, level):
        inverse = 1.0 / rho
        equil = equilibrium(rho, [m * inverse for m in mom])
        departure = [f[i] - equil[i] for i in range(27)]
        projected = along_axes(departure, to_moments)
        fluid = along_axes([projected[a] * (-rates[a]) for a in range(27)], from_moments)
        for i in range(27):
            keep[i, level] = f[i] + fluid[i]
            mix[i, level] = departure[26 - i] - f[i] - fluid[i]

    loads[4].wait()
    loads[5].wait()
    first = []
    for level in range(2):
        f = [pop[i, level] for i in range(27)]
        rho, mom = moments(f)
        first.append((rho, mom))
        collide(f, rho, mom, level)

    wait_all(send_m, recv_m, a_recv.at[0])
    diag = iota((CAP, 128), 0) == iota((CAP, 128), 1) % CAP
    spread = jnp.concatenate(
        [
            jnp.where(diag, jnp.broadcast_to(recv_m[s : s + 1, :], (CAP, 128)), 0.0)
            for s in range(DEV)
        ],
        axis=0,
    ).astype(BF16)
    sel = one_hot(iota((CAP, 128), 0) == iota((CAP, 128), 1) // CAP)
    info = nt(sel, spread)
    match = jnp.where(iota((16, SLOTS), 0, F32) == info[0:1], 1.0, 0.0)
    match_s[...] = match
    weights = jnp.concatenate(
        [match] + [match * info[k : k + 1] for k in range(1, 4)], axis=0
    ).astype(BF16)

    wait_all(send_f, recv_f, a_recv.at[1])
    summed = nn(weights, recv_f[...].reshape(SLOTS, 128))
    covers = []
    for level in range(2):
        at = lambda k: summed[16 * k + 8 * level : 16 * k + 8 * level + 8]
        solid = at(0)
        inverse = 1.0 / (1.0 + solid)
        covers.append((inverse, solid * inverse, [at(k) * inverse for k in range(1, 4)]))

    up, down = gz < 3, gz > 0
    right, left = lax.rem(gx + 1, 32), lax.rem(gx + 31, 32)
    sub = iota((8, 128), 0)

    def halo(step):
        def copy(k, src, dst, device):
            return pltpu.make_async_remote_copy(
                src_ref=src,
                dst_ref=dst,
                send_sem=h_send.at[k],
                recv_sem=h_recv.at[step, k],
                device_id=device,
                device_id_type=MESH,
            )

        def edge(k, side, row, rows, device):
            at = (step, side, slice(None), pl.ds(row, rows))
            return copy(k, edge_s.at[at], edge_r.at[at], device)

        return (
            [edge(0, 0, 0, 4, (gz, right)), edge(0, 1, 0, 4, (gz, left))],
            [edge(1, 0, 4, 1, (gz + 1, right)), edge(1, 1, 4, 1, (gz + 1, left))],
            [edge(2, 0, 5, 1, (gz - 1, right)), edge(2, 1, 5, 1, (gz - 1, left))],
            [copy(3, z_s.at[step, 0], z_r.at[step, 0], (gz + 1, gx))],
            [copy(4, z_s.at[step, 1], z_r.at[step, 1], (gz - 1, gx))],
        )

    def wait_bytes(step, k, sem):
        if k < 3:
            at = (step, slice(None), slice(None), pl.ds(*((0, 4), (4, 1), (5, 1))[k]))
            src, dst = edge_s.at[at], edge_r.at[at]
        else:
            src, dst = z_s.at[step, k - 3], z_r.at[step, k - 3]
        pltpu.make_async_copy(src, dst, sem).wait()

    sends = (None, up, down, up, down)
    comes = (None, down, up, down, up)

    def guarded(test, run):
        if test is None:
            run()
        else:
            pl.when(test)(run)

    def start(copies, groups):
        for k in groups:
            guarded(sends[k], lambda k=k: [c.start() for c in copies[k]] and None)

    def arrive(step, groups):
        for k in groups:
            guarded(comes[k], lambda k=k: wait_bytes(step, k, h_recv.at[step, k]))

    def sent(step):
        for k in range(5):
            guarded(sends[k], lambda k=k: wait_bytes(step, k, h_send.at[k]))

    def edge_row(i, origin):
        cz = VEL[i][0]
        if cz == 0:
            return origin
        if cz > 0:
            return 2 if origin == 0 else 4
        return 3 if origin == 1 else 5

    def shifted(value, i):
        _, cx, cy = VEL[i]
        if cx:
            value = pltpu.roll(value, cx % 8, 0)
            value = jnp.where(sub == (0 if cx > 0 else 7), 0.0, value)
        if cy:
            value = pltpu.roll(value, cy % 128, 1)
        return value

    def leave(step, rhos):
        copies = halo(step)
        equils = [equilibrium(rhos[level], covers[level][2]) for level in range(2)]

        def finish(i, level):
            value = keep[i, level] + covers[level][1] * (mix[i, level] + equils[level][i])
            post[i, level] = value
            return value

        for i in range(27):
            cx, cy = VEL[i][1:]
            if cx:
                for level in range(2):
                    value = finish(i, level)
                    side, row = (0, 7) if cx > 0 else (1, 0)
                    k = edge_row(i, level)
                    edge_s[step, side, cy + 1, k : k + 1, :] = value[row : row + 1]
        start(copies, (1, 2, 0))
        for i in range(27):
            if VEL[i][1] == 0:
                for level in range(2):
                    finish(i, level)
        for i in range(9):
            z_s[step, 0, i] = shifted(post[18 + i, 1], 18 + i)
            z_s[step, 1, i] = shifted(post[i, 0], i)
        start(copies, (3, 4))

    def inside(out):
        for i in range(27):
            for level in range(2):
                if 0 <= level - VEL[i][0] <= 1:
                    out[i, level] = shifted(post[i, level - VEL[i][0]], i)

    def through_walls(step, out):
        for i in range(9):
            out[18 + i, 0] = jnp.where(gz == 0, post[8 - i, 0], z_r[step, 0, i])
            out[i, 1] = jnp.where(gz == 3, post[26 - i, 1], z_r[step, 1, i])

    def moved_edges(step):
        return [
            [
                edge_r[step, side, cy + 1]
                if cy == 0
                else pltpu.roll(edge_r[step, side, cy + 1], cy % 128, 1)
                for cy in (-1, 0, 1)
            ]
            for side in range(2)
        ]

    def edge_values(edges, level):
        for i in range(27):
            cz, cx, cy = VEL[i]
            if cx:
                side = 0 if cx > 0 else 1
                origin = level - cz
                if origin < 0 or origin > 1:
                    k, wall = (4, gz == 0) if cz > 0 else (5, gz == 3)
                else:
                    k, wall = edge_row(i, origin), None
                row = edges[side][cy + 1][k : k + 1]
                yield i, (0 if cx > 0 else 7), row, wall

    leave(0, [first[level][0] for level in range(2)])
    inside(cells)
    partial = []
    for level in range(2):
        f = [
            cells[i, level] if 0 <= level - VEL[i][0] <= 1 else None for i in range(27)
        ]
        partial.append(moments(f))
    arrive(0, (3, 4))
    through_walls(0, cells)
    for level in range(2):
        f = [
            None if 0 <= level - VEL[i][0] <= 1 else cells[i, level] for i in range(27)
        ]
        partial[level] = add_moments(partial[level], moments(f))
    arrive(0, (0, 1, 2))
    edges = moved_edges(0)
    fixes = []
    for level in range(2):
        f = {0: [None] * 27, 7: [None] * 27}
        for i, x, row, wall in edge_values(edges, level):
            if wall is not None:
                row = jnp.where(wall, 0.0, row)
            f[x][i] = jnp.broadcast_to(row, (8, 128))
        for x in (0, 7):
            rho, mom = moments(f[x])
            here = sub == x
            extra = (jnp.where(here, rho, 0.0), [jnp.where(here, m, 0.0) for m in mom])
            partial[level] = add_moments(partial[level], extra)
    second = partial
    pushes = [[None, None] for _ in range(3)]
    for level in range(2):
        rho, mom = second[level]
        inverse, _, us = covers[level]
        rho_sum = first[level][0] + rho
        for k in range(3):
            pushes[k][level] = ((first[level][1][k] + mom[k]) - us[k] * rho_sum) * inverse

    push = jnp.concatenate([pushes[k][level] for k in range(3) for level in range(2)], axis=0)
    high, low = split(push)
    grains = recv_f[...].reshape(SLOTS, 128)
    all_lines = nt(high, grains) + nt(low, grains)
    match = match_s[...]
    diag = iota((CAP, SLOTS), 0) == iota((CAP, SLOTS), 1) % CAP
    parts = []
    for k in range(3):
        force = jnp.sum(match * all_lines[16 * k : 16 * k + 16], axis=0, keepdims=True)
        parts.append(jnp.where(diag, force, 0.0))
    halves = split(jnp.concatenate(parts, axis=0))
    owner = one_hot(iota((DEV, SLOTS), 0) == iota((DEV, SLOTS), 1) // CAP)
    both = jnp.concatenate([h.astype(F32) for h in halves] + [jnp.zeros((DEV - 48, SLOTS), F32)], axis=0)
    send_r[...] = nt(owner, both.astype(BF16))
    recv_r[pl.ds(me, 1), :] = send_r[pl.ds(me, 1), :]
    for o in OFFSETS:
        to_peer(o, send_r, recv_r, 2, False)

    for level in range(2):
        for i, x, row, wall in edge_values(edges, level):
            if wall is not None:
                row = jnp.where(wall, cells[i, level, x : x + 1, :], row)
            cells[i, level, x : x + 1, :] = row
    for level in range(2):
        f = [cells[i, level] for i in range(27)]
        rho, mom = second[level]
        collide(f, rho, mom, level)
    sent(0)
    leave(1, [second[level][0] for level in range(2)])
    inside(f_out)
    arrive(1, (3, 4))
    through_walls(1, f_out)
    arrive(1, (0, 1, 2))
    edges = moved_edges(1)
    for level in range(2):
        for i, x, row, wall in edge_values(edges, level):
            if wall is not None:
                row = jnp.where(wall, f_out[i, level, x : x + 1, :], row)
            f_out[i, level, x : x + 1, :] = row
    for i in range(27):
        for level in range(2):
            f_out[i, level] = f_out[i, level] * (1.0 / WEIGHT[i])

    wait_all(send_r, recv_r, a_recv.at[2])
    table = recv_r[...].T[0 : 6 * CAP].astype(BF16)
    per_grain = nn(table, chosen_s[...])
    rank_mask = rank_s[...]
    for k in range(3):
        at = CAP * k
        total = per_grain[at : at + CAP] + per_grain[24 + at : 24 + at + CAP]
        force_out[k : k + 1, :] = jnp.sum(rank_mask * total, axis=0, keepdims=True)

    wait_all(send_m, recv_m, a_send.at[0])
    wait_all(send_f, recv_f, a_send.at[1])
    wait_all(send_r, recv_r, a_send.at[2])
    sent(1)


def write_out(cells, force, cells_out, force_out, sem):
    copies = [
        pltpu.make_async_copy(cells, cells_out, sem.at[0]),
        pltpu.make_async_copy(force, force_out, sem.at[1]),
    ]
    for c in copies:
        c.start()
    for c in copies:
        c.wait()


def per_device(populations, rates, grain_fraction, grain_velocity, grain_dest, grain_line):
    hbm = pl.BlockSpec(memory_space=pl.ANY)
    vmem = pl.BlockSpec(memory_space=pltpu.VMEM)
    dma = pltpu.SemaphoreType.DMA
    block = (27, 2, 8, 128)
    cells, force = pl.pallas_call(
        kernel,
        out_shape=(
            pltpu.VMEM(block, F32),
            pltpu.VMEM((3, GRAINS), F32),
        ),
        in_specs=[hbm] * 6,
        out_specs=(vmem, vmem),
        scratch_shapes=[
            pltpu.SMEM((27,), F32),
            pltpu.VMEM(block, F32),
            pltpu.VMEM((GRAINS, 128), BF16),
            pltpu.VMEM((3, GRAINS), BF16),
            pltpu.VMEM((1, GRAINS), jnp.int32),
            pltpu.VMEM((1, GRAINS), jnp.int32),
            pltpu.VMEM((DEV, CAP, 128), BF16),
            pltpu.VMEM((DEV, 128), F32),
            pltpu.VMEM((DEV, CAP, 128), BF16),
            pltpu.VMEM((DEV, 128), F32),
            pltpu.VMEM((DEV, 128), F32),
            pltpu.VMEM((DEV, 128), F32),
            pltpu.VMEM(block, F32),
            pltpu.VMEM(block, F32),
            pltpu.VMEM(block, F32),
            pltpu.VMEM((2, 2, 3, 8, 128), F32),
            pltpu.VMEM((2, 2, 3, 8, 128), F32),
            pltpu.VMEM((2, 2, 9, 8, 128), F32),
            pltpu.VMEM((2, 2, 9, 8, 128), F32),
            pltpu.VMEM((DEV, GRAINS), BF16),
            pltpu.VMEM((CAP, GRAINS), F32),
            pltpu.VMEM((16, SLOTS), F32),
            pltpu.VMEM(block, F32),
            dma((6,)),
            dma((3,)),
            dma((3,)),
            dma((5,)),
            dma((2, 5)),
        ],
        compiler_params=pltpu.CompilerParams(collective_id=0, has_side_effects=True),
        name="lattice",
    )(
        populations,
        rates,
        grain_fraction,
        grain_velocity,
        grain_dest.reshape(1, GRAINS),
        grain_line.reshape(1, GRAINS),
    )
    return pl.pallas_call(
        write_out,
        out_shape=(jax.ShapeDtypeStruct(block, F32), jax.ShapeDtypeStruct((3, GRAINS), F32)),
        in_specs=[hbm, hbm],
        out_specs=(hbm, hbm),
        scratch_shapes=[dma((2,))],
        compiler_params=pltpu.CompilerParams(vmem_limit_bytes=1 << 20),
        name="write_out",
    )(cells, force)


def solution(mesh):
    in_specs = (
        P(None, "gz", "gx", None),
        P(),
        P(("gz", "gx"), None),
        P(None, ("gz", "gx")),
        P(("gz", "gx"), None),
        P(("gz", "gx")),
    )
    out_specs = (P(None, "gz", "gx", None), P(None, ("gz", "gx")))
    return jax.shard_map(
        per_device, mesh=mesh, in_specs=in_specs, out_specs=out_specs, check_vma=False
    )
```

```python
import functools
import itertools

import jax
import jax.numpy as jnp
from jax import lax
from jax.experimental import pallas as pl
from jax.experimental.pallas import tpu as pltpu
from jax.sharding import PartitionSpec as P

MESH = pl.DeviceIdType.MESH
F32 = jnp.float32
BF16 = jnp.bfloat16
DEV = 128
CAP = 8
GRAINS = 512
SLOTS = DEV * CAP
VEL = [(i // 9 - 1, i // 3 % 3 - 1, i % 3 - 1) for i in range(27)]
WEIGHT = [(8.0 / 27, 2.0 / 27, 1.0 / 54, 1.0 / 216)[sum(map(abs, c))] for c in VEL]
NT = (((1,), (1,)), ((), ()))


def ring(v):
    return min(v, 4 - v)


OFFSETS = sorted(
    (o for o in itertools.product(range(4), range(4), range(4), range(2)) if any(o)),
    key=lambda o: -(0.75 * (ring(o[0]) + ring(o[1]) + ring(o[2])) + 0.5 * sum(v > 0 for v in o[:3]) + 0.2 * o[3]),
)


def iota(shape, dim, dtype=jnp.int32):
    out = lax.broadcasted_iota(jnp.int32, shape, dim)
    return out if dtype == jnp.int32 else out.astype(dtype)


def one_hot(mask):
    return jnp.where(mask, 1.0, 0.0).astype(BF16)


def split(x):
    high = x.astype(BF16)
    low = (x - high.astype(F32)).astype(BF16)
    return high, low


def nt(a, b):
    return lax.dot_general(a, b, NT, preferred_element_type=F32)


def nn(a, b):
    return jnp.dot(a, b, preferred_element_type=F32)


def along_axes(values, triple):
    for stride in (1, 3, 9):
        out = [None] * 27
        for base in range(27):
            if base // stride % 3 == 0:
                idx = (base, base + stride, base + 2 * stride)
                for k, v in zip(idx, triple(*(values[j] for j in idx))):
                    out[k] = v
        values = out
    return values


def to_moments(a, b, c):
    s = a + c
    return s + b, c - a, s


def from_moments(m0, m1, m2):
    h0, h1 = 0.5 * m2, 0.5 * m1
    return h0 - h1, m0 - m2, h0 + h1


def moments(f):
    plane = {}
    for i in range(27):
        if f[i] is not None:
            for key in [None] + [(k, VEL[i][k]) for k in range(3) if VEL[i][k]]:
                plane[key] = f[i] if key not in plane else plane[key] + f[i]

    def along(k):
        if (k, 1) not in plane:
            return -plane[(k, -1)] if (k, -1) in plane else jnp.zeros_like(plane[None])
        return plane[(k, 1)] - plane[(k, -1)] if (k, -1) in plane else plane[(k, 1)]

    return plane[None], [along(k) for k in range(3)]


def add_moments(a, b):
    return a[0] + b[0], [p + q for p, q in zip(a[1], b[1])]


def equilibrium(rho, v):
    t = [3.0 * q for q in v]
    base = rho * (1.0 - 1.5 * (v[0] * v[0] + v[1] * v[1] + v[2] * v[2]))
    half = 0.5 * rho
    out = [None] * 27
    for i in range(13):
        along = None
        c = VEL[26 - i]
        for k in range(3):
            if c[k]:
                term = t[k]
                if along is None:
                    along = term if c[k] > 0 else -term
                else:
                    along = along + term if c[k] > 0 else along - term
        even = base + half * (along * along)
        odd = rho * along
        out[26 - i] = WEIGHT[i] * (even + odd)
        out[i] = WEIGHT[i] * (even - odd)
    out[13] = WEIGHT[13] * base
    return out


def kernel(
    pop_in, rates_in, frac_in, vel_in, dest_in, line_in,
    f_out, table_out, chosen_s, rank_s,
    rates, pop, frac, vel, dest, line,
    send_f, send_m, recv_f, recv_m, send_r, recv_r,
    keep, mix, post, edge_s, edge_r, z_s, z_r,
    match_s, cells,
    a_send, a_recv, h_send, h_recv,
):
    gz, gx = lax.axis_index("gz"), lax.axis_index("gx")
    me = gz * 32 + gx
    yy, zz, core = gx // 8, gx // 2 % 4, gx % 2
    at_x = [lax.rem(gz + a, 4) for a in range(4)]
    at_y = [lax.rem(yy + b, 4) * 8 for b in range(4)]
    at_z = [lax.rem(zz + c, 4) * 2 for c in range(4)]
    at_core = [core, 1 - core]

    def peer(o):
        return at_x[o[0]], at_y[o[1]] + (at_z[o[2]] + at_core[o[3]])

    barrier = pltpu.get_barrier_semaphore()
    for o in OFFSETS:
        pl.semaphore_signal(barrier, inc=1, device_id=peer(o), device_id_type=MESH)

    loads = [
        pltpu.make_async_copy(src, dst, sem)
        for src, dst, sem in (
            (dest_in, dest, h_send.at[0]),
            (line_in, line, h_send.at[1]),
            (vel_in, vel, h_send.at[2]),
            (frac_in, frac, a_send.at[1]),
            (pop_in, pop, h_send.at[3]),
            (rates_in, rates, h_send.at[4]),
        )
    ]
    for load in loads:
        load.start()

    earlier = one_hot(iota((GRAINS, GRAINS), 0) < iota((GRAINS, GRAINS), 1))
    loads[0].wait()
    target = dest[...]
    chosen = iota((DEV, GRAINS), 0) == target
    chosen_b = one_hot(chosen)
    chosen_s[...] = chosen_b
    before = nn(chosen_b, earlier)
    rank = jnp.sum(jnp.where(chosen, before, 0.0), axis=0, keepdims=True)
    rank_mask = jnp.where(iota((CAP, GRAINS), 0, F32) == rank, 1.0, 0.0)
    rank_s[...] = rank_mask

    loads[1].wait()
    loads[2].wait()
    speed = vel[...].astype(F32)
    values = [line[...].astype(F32)] + [speed[k : k + 1] for k in range(3)]
    rows = [rank_mask * v for v in values] + [jnp.zeros((DEV - 4 * CAP, GRAINS), F32)]
    send_m[...] = nt(chosen_b, jnp.concatenate(rows, axis=0).astype(BF16))

    loads[3].wait()
    place = target.astype(F32) * CAP + rank
    fractions = frac[...]
    for j in range(8):
        pick = one_hot(iota((128, GRAINS), 0, F32) + 128.0 * j == place)
        send_f[16 * j : 16 * j + 16] = nn(pick, fractions).astype(BF16).reshape(16, CAP, 128)
    recv_m[pl.ds(me, 1), :] = send_m[pl.ds(me, 1), :]
    recv_f[me] = send_f[me]

    pl.semaphore_wait(barrier, DEV - 1)

    def to_peer(o, src, dst, k, wide):
        d = peer(o)
        p = d[0] * 32 + d[1]
        pltpu.make_async_remote_copy(
            src_ref=src.at[p] if wide else src.at[pl.ds(p, 1)],
            dst_ref=dst.at[me] if wide else dst.at[pl.ds(me, 1)],
            send_sem=a_send.at[k],
            recv_sem=a_recv.at[k],
            device_id=d,
            device_id_type=MESH,
        ).start()

    def wait_all(src, dst, sem):
        pltpu.make_async_copy(src.at[pl.ds(0, DEV - 1)], dst.at[pl.ds(0, DEV - 1)], sem).wait()

    for o in OFFSETS:
        to_peer(o, send_m, recv_m, 0, False)
        to_peer(o, send_f, recv_f, 1, True)

    def collide(f, rho, mom, level):
        inverse = 1.0 / rho
        equil = equilibrium(rho, [m * inverse for m in mom])
        departure = [f[i] - equil[i] for i in range(27)]
        projected = along_axes(departure, to_moments)
        fluid = along_axes([projected[a] * (-rates[a]) for a in range(27)], from_moments)
        for i in range(27):
            keep[i, level] = f[i] + fluid[i]
            mix[i, level] = departure[26 - i] - f[i] - fluid[i]

    loads[4].wait()
    loads[5].wait()
    first = []
    for level in range(2):
        f = [pop[i, level] for i in range(27)]
        rho, mom = moments(f)
        first.append((rho, mom))
        collide(f, rho, mom, level)

    wait_all(send_m, recv_m, a_recv.at[0])
    diag = iota((CAP, 128), 0) == iota((CAP, 128), 1) % CAP
    spread = jnp.concatenate(
        [
            jnp.where(diag, jnp.broadcast_to(recv_m[s : s + 1, :], (CAP, 128)), 0.0)
            for s in range(DEV)
        ],
        axis=0,
    ).astype(BF16)
    sel = one_hot(iota((CAP, 128), 0) == iota((CAP, 128), 1) // CAP)
    info = nt(sel, spread)
    match = jnp.where(iota((16, SLOTS), 0, F32) == info[0:1], 1.0, 0.0)
    match_s[...] = match
    weights = jnp.concatenate(
        [match] + [match * info[k : k + 1] for k in range(1, 4)], axis=0
    ).astype(BF16)

    wait_all(send_f, recv_f, a_recv.at[1])
    summed = nn(weights, recv_f[...].reshape(SLOTS, 128))
    covers = []
    for level in range(2):
        at = lambda k: summed[16 * k + 8 * level : 16 * k + 8 * level + 8]
        solid = at(0)
        inverse = 1.0 / (1.0 + solid)
        covers.append((inverse, solid * inverse, [at(k) * inverse for k in range(1, 4)]))

    up, down = gz < 3, gz > 0
    right, left = lax.rem(gx + 1, 32), lax.rem(gx + 31, 32)
    sub = iota((8, 128), 0)

    def halo(step):
        def copy(k, src, dst, device):
            return pltpu.make_async_remote_copy(
                src_ref=src,
                dst_ref=dst,
                send_sem=h_send.at[k],
                recv_sem=h_recv.at[step, k],
                device_id=device,
                device_id_type=MESH,
            )

        def edge(k, side, row, rows, device):
            at = (step, side, slice(None), pl.ds(row, rows))
            return copy(k, edge_s.at[at], edge_r.at[at], device)

        return (
            [edge(0, 0, 0, 4, (gz, right)), edge(0, 1, 0, 4, (gz, left))],
            [edge(1, 0, 4, 1, (gz + 1, right)), edge(1, 1, 4, 1, (gz + 1, left))],
            [edge(2, 0, 5, 1, (gz - 1, right)), edge(2, 1, 5, 1, (gz - 1, left))],
            [copy(3, z_s.at[step, 0], z_r.at[step, 0], (gz + 1, gx))],
            [copy(4, z_s.at[step, 1], z_r.at[step, 1], (gz - 1, gx))],
        )

    def wait_bytes(step, k, sem):
        if k < 3:
            at = (step, slice(None), slice(None), pl.ds(*((0, 4), (4, 1), (5, 1))[k]))
            src, dst = edge_s.at[at], edge_r.at[at]
        else:
            src, dst = z_s.at[step, k - 3], z_r.at[step, k - 3]
        pltpu.make_async_copy(src, dst, sem).wait()

    sends = (None, up, down, up, down)
    comes = (None, down, up, down, up)

    def guarded(test, run):
        if test is None:
            run()
        else:
            pl.when(test)(run)

    def start(copies, groups):
        for k in groups:
            guarded(sends[k], lambda k=k: [c.start() for c in copies[k]] and None)

    def arrive(step, groups):
        for k in groups:
            guarded(comes[k], lambda k=k: wait_bytes(step, k, h_recv.at[step, k]))

    def sent(step):
        for k in range(5):
            guarded(sends[k], lambda k=k: wait_bytes(step, k, h_send.at[k]))

    def edge_row(i, origin):
        cz = VEL[i][0]
        if cz == 0:
            return origin
        if cz > 0:
            return 2 if origin == 0 else 4
        return 3 if origin == 1 else 5

    def shifted(value, i):
        _, cx, cy = VEL[i]
        if cx:
            value = pltpu.roll(value, cx % 8, 0)
            value = jnp.where(sub == (0 if cx > 0 else 7), 0.0, value)
        if cy:
            value = pltpu.roll(value, cy % 128, 1)
        return value

    def leave(step, rhos):
        copies = halo(step)
        equils = [equilibrium(rhos[level], covers[level][2]) for level in range(2)]

        def finish(i, level):
            value = keep[i, level] + covers[level][1] * (mix[i, level] + equils[level][i])
            post[i, level] = value
            return value

        for i in range(27):
            cx, cy = VEL[i][1:]
            if cx:
                for level in range(2):
                    value = finish(i, level)
                    side, row = (0, 7) if cx > 0 else (1, 0)
                    k = edge_row(i, level)
                    edge_s[step, side, cy + 1, k : k + 1, :] = value[row : row + 1]
        start(copies, (1, 2, 0))
        for i in range(27):
            if VEL[i][1] == 0:
                for level in range(2):
                    finish(i, level)
        for i in range(9):
            z_s[step, 0, i] = shifted(post[18 + i, 1], 18 + i)
            z_s[step, 1, i] = shifted(post[i, 0], i)
        start(copies, (3, 4))

    def inside(out):
        for i in range(27):
            for level in range(2):
                if 0 <= level - VEL[i][0] <= 1:
                    out[i, level] = shifted(post[i, level - VEL[i][0]], i)

    def through_walls(step, out):
        for i in range(9):
            out[18 + i, 0] = jnp.where(gz == 0, post[8 - i, 0], z_r[step, 0, i])
            out[i, 1] = jnp.where(gz == 3, post[26 - i, 1], z_r[step, 1, i])

    def moved_edges(step):
        return [
            [
                edge_r[step, side, cy + 1]
                if cy == 0
                else pltpu.roll(edge_r[step, side, cy + 1], cy % 128, 1)
                for cy in (-1, 0, 1)
            ]
            for side in range(2)
        ]

    def edge_values(edges, level):
        for i in range(27):
            cz, cx, cy = VEL[i]
            if cx:
                side = 0 if cx > 0 else 1
                origin = level - cz
                if origin < 0 or origin > 1:
                    k, wall = (4, gz == 0) if cz > 0 else (5, gz == 3)
                else:
                    k, wall = edge_row(i, origin), None
                row = edges[side][cy + 1][k : k + 1]
                yield i, (0 if cx > 0 else 7), row, wall

    leave(0, [first[level][0] for level in range(2)])
    inside(cells)
    partial = []
    for level in range(2):
        f = [
            cells[i, level] if 0 <= level - VEL[i][0] <= 1 else None for i in range(27)
        ]
        partial.append(moments(f))
    arrive(0, (3, 4))
    through_walls(0, cells)
    for level in range(2):
        f = [
            None if 0 <= level - VEL[i][0] <= 1 else cells[i, level] for i in range(27)
        ]
        partial[level] = add_moments(partial[level], moments(f))
    arrive(0, (0, 1, 2))
    edges = moved_edges(0)
    fixes = []
    for level in range(2):
        f = {0: [None] * 27, 7: [None] * 27}
        for i, x, row, wall in edge_values(edges, level):
            if wall is not None:
                row = jnp.where(wall, 0.0, row)
            f[x][i] = jnp.broadcast_to(row, (8, 128))
        for x in (0, 7):
            rho, mom = moments(f[x])
            here = sub == x
            extra = (jnp.where(here, rho, 0.0), [jnp.where(here, m, 0.0) for m in mom])
            partial[level] = add_moments(partial[level], extra)
    second = partial
    pushes = [[None, None] for _ in range(3)]
    for level in range(2):
        rho, mom = second[level]
        inverse, _, us = covers[level]
        rho_sum = first[level][0] + rho
        for k in range(3):
            pushes[k][level] = ((first[level][1][k] + mom[k]) - us[k] * rho_sum) * inverse

    for level in range(1):
        for i, x, row, wall in edge_values(edges, level):
            if wall is not None:
                row = jnp.where(wall, cells[i, level, x : x + 1, :], row)
            cells[i, level, x : x + 1, :] = row
    for level in range(1):
        f = [cells[i, level] for i in range(27)]
        rho, mom = second[level]
        collide(f, rho, mom, level)

    push = jnp.concatenate([pushes[k][level] for k in range(3) for level in range(2)], axis=0)
    high, low = split(push)
    grains = recv_f[...].reshape(SLOTS, 128)
    all_lines = nt(high, grains) + nt(low, grains)
    match = match_s[...]
    diag = iota((CAP, SLOTS), 0) == iota((CAP, SLOTS), 1) % CAP
    parts = []
    for k in range(3):
        force = jnp.sum(match * all_lines[16 * k : 16 * k + 16], axis=0, keepdims=True)
        parts.append(jnp.where(diag, force, 0.0))
    halves = split(jnp.concatenate(parts, axis=0))
    owner = one_hot(iota((DEV, SLOTS), 0) == iota((DEV, SLOTS), 1) // CAP)
    both = jnp.concatenate([h.astype(F32) for h in halves] + [jnp.zeros((DEV - 48, SLOTS), F32)], axis=0)
    send_r[...] = nt(owner, both.astype(BF16))
    recv_r[pl.ds(me, 1), :] = send_r[pl.ds(me, 1), :]
    for o in OFFSETS:
        to_peer(o, send_r, recv_r, 2, False)

    for level in range(1, 2):
        for i, x, row, wall in edge_values(edges, level):
            if wall is not None:
                row = jnp.where(wall, cells[i, level, x : x + 1, :], row)
            cells[i, level, x : x + 1, :] = row
    for level in range(1, 2):
        f = [cells[i, level] for i in range(27)]
        rho, mom = second[level]
        collide(f, rho, mom, level)
    sent(0)
    leave(1, [second[level][0] for level in range(2)])
    inside(f_out)
    arrive(1, (3, 4))
    through_walls(1, f_out)
    arrive(1, (0, 1, 2))
    edges = moved_edges(1)
    for level in range(2):
        for i, x, row, wall in edge_values(edges, level):
            if wall is not None:
                row = jnp.where(wall, f_out[i, level, x : x + 1, :], row)
            f_out[i, level, x : x + 1, :] = row
    for i in range(27):
        for level in range(2):
            f_out[i, level] = f_out[i, level] * (1.0 / WEIGHT[i])

    wait_all(send_r, recv_r, a_recv.at[2])
    table_out[...] = recv_r[...]

    wait_all(send_m, recv_m, a_send.at[0])
    wait_all(send_f, recv_f, a_send.at[1])
    wait_all(send_r, recv_r, a_send.at[2])
    sent(1)


def write_out(cells, table_in, chosen_in, rank_in, cells_out, force_out, force, sem):
    first = pltpu.make_async_copy(cells, cells_out, sem.at[0])
    first.start()
    table = table_in[...].T[0 : 6 * CAP].astype(BF16)
    per_grain = nn(table, chosen_in[...])
    rank_mask = rank_in[...]
    for k in range(3):
        at = CAP * k
        total = per_grain[at : at + CAP] + per_grain[24 + at : 24 + at + CAP]
        force[k : k + 1, :] = jnp.sum(rank_mask * total, axis=0, keepdims=True)
    second = pltpu.make_async_copy(force, force_out, sem.at[1])
    second.start()
    first.wait()
    second.wait()


def per_device(populations, rates, grain_fraction, grain_velocity, grain_dest, grain_line):
    hbm = pl.BlockSpec(memory_space=pl.ANY)
    vmem = pl.BlockSpec(memory_space=pltpu.VMEM)
    dma = pltpu.SemaphoreType.DMA
    block = (27, 2, 8, 128)
    parts = pl.pallas_call(
        kernel,
        out_shape=(
            pltpu.VMEM(block, F32),
            pltpu.VMEM((DEV, 128), F32),
            pltpu.VMEM((DEV, GRAINS), BF16),
            pltpu.VMEM((CAP, GRAINS), F32),
        ),
        in_specs=[hbm] * 6,
        out_specs=(vmem,) * 4,
        scratch_shapes=[
            pltpu.SMEM((27,), F32),
            pltpu.VMEM(block, F32),
            pltpu.VMEM((GRAINS, 128), BF16),
            pltpu.VMEM((3, GRAINS), BF16),
            pltpu.VMEM((1, GRAINS), jnp.int32),
            pltpu.VMEM((1, GRAINS), jnp.int32),
            pltpu.VMEM((DEV, CAP, 128), BF16),
            pltpu.VMEM((DEV, 128), F32),
            pltpu.VMEM((DEV, CAP, 128), BF16),
            pltpu.VMEM((DEV, 128), F32),
            pltpu.VMEM((DEV, 128), F32),
            pltpu.VMEM((DEV, 128), F32),
            pltpu.VMEM(block, F32),
            pltpu.VMEM(block, F32),
            pltpu.VMEM(block, F32),
            pltpu.VMEM((2, 2, 3, 8, 128), F32),
            pltpu.VMEM((2, 2, 3, 8, 128), F32),
            pltpu.VMEM((2, 2, 9, 8, 128), F32),
            pltpu.VMEM((2, 2, 9, 8, 128), F32),
            pltpu.VMEM((16, SLOTS), F32),
            pltpu.VMEM(block, F32),
            dma((3,)),
            dma((3,)),
            dma((5,)),
            dma((2, 5)),
        ],
        compiler_params=pltpu.CompilerParams(collective_id=0, has_side_effects=True),
        name="lattice",
    )(
        populations,
        rates,
        grain_fraction,
        grain_velocity,
        grain_dest.reshape(1, GRAINS),
        grain_line.reshape(1, GRAINS),
    )
    return pl.pallas_call(
        write_out,
        out_shape=(jax.ShapeDtypeStruct(block, F32), jax.ShapeDtypeStruct((3, GRAINS), F32)),
        in_specs=[hbm, vmem, vmem, vmem],
        out_specs=(hbm, hbm),
        scratch_shapes=[pltpu.VMEM((3, GRAINS), F32), dma((2,))],
        compiler_params=pltpu.CompilerParams(vmem_limit_bytes=1 << 20),
        name="write_out",
    )(*parts)


def solution(mesh):
    in_specs = (
        P(None, "gz", "gx", None),
        P(),
        P(("gz", "gx"), None),
        P(None, ("gz", "gx")),
        P(("gz", "gx"), None),
        P(("gz", "gx")),
    )
    out_specs = (P(None, "gz", "gx", None), P(None, ("gz", "gx")))
    return jax.shard_map(
        per_device, mesh=mesh, in_specs=in_specs, out_specs=out_specs, check_vma=False
    )
```

```python
import functools
import itertools

import jax
import jax.numpy as jnp
from jax import lax
from jax.experimental import pallas as pl
from jax.experimental.pallas import tpu as pltpu
from jax.sharding import PartitionSpec as P

MESH = pl.DeviceIdType.MESH
F32 = jnp.float32
BF16 = jnp.bfloat16
DEV = 128
CAP = 8
GRAINS = 512
SLOTS = DEV * CAP
VEL = [(i // 9 - 1, i // 3 % 3 - 1, i % 3 - 1) for i in range(27)]
WEIGHT = [(8.0 / 27, 2.0 / 27, 1.0 / 54, 1.0 / 216)[sum(map(abs, c))] for c in VEL]
NT = (((1,), (1,)), ((), ()))


def ring(v):
    return min(v, 4 - v)


OFFSETS = sorted(
    (o for o in itertools.product(range(4), range(4), range(4), range(2)) if any(o)),
    key=lambda o: -(0.75 * (ring(o[0]) + ring(o[1]) + ring(o[2])) + 0.5 * sum(v > 0 for v in o[:3]) + 0.2 * o[3]),
)


LEAD = 32


def iota(shape, dim, dtype=jnp.int32):
    out = lax.broadcasted_iota(jnp.int32, shape, dim)
    return out if dtype == jnp.int32 else out.astype(dtype)


def one_hot(mask):
    return jnp.where(mask, 1.0, 0.0).astype(BF16)


def split(x):
    high = x.astype(BF16)
    low = (x - high.astype(F32)).astype(BF16)
    return high, low


def nt(a, b):
    return lax.dot_general(a, b, NT, preferred_element_type=F32)


def nn(a, b):
    return jnp.dot(a, b, preferred_element_type=F32)


def along_axes(values, triple):
    for stride in (1, 3, 9):
        out = [None] * 27
        for base in range(27):
            if base // stride % 3 == 0:
                idx = (base, base + stride, base + 2 * stride)
                for k, v in zip(idx, triple(*(values[j] for j in idx))):
                    out[k] = v
        values = out
    return values


def to_moments(a, b, c):
    s = a + c
    return s + b, c - a, s


def from_moments(m0, m1, m2):
    h0, h1 = 0.5 * m2, 0.5 * m1
    return h0 - h1, m0 - m2, h0 + h1


def moments(f):
    plane = {}
    for i in range(27):
        if f[i] is not None:
            for key in [None] + [(k, VEL[i][k]) for k in range(3) if VEL[i][k]]:
                plane[key] = f[i] if key not in plane else plane[key] + f[i]

    def along(k):
        if (k, 1) not in plane:
            return -plane[(k, -1)] if (k, -1) in plane else jnp.zeros_like(plane[None])
        return plane[(k, 1)] - plane[(k, -1)] if (k, -1) in plane else plane[(k, 1)]

    return plane[None], [along(k) for k in range(3)]


def add_moments(a, b):
    return a[0] + b[0], [p + q for p, q in zip(a[1], b[1])]


def equilibrium(rho, v):
    t = [3.0 * q for q in v]
    base = rho * (1.0 - 1.5 * (v[0] * v[0] + v[1] * v[1] + v[2] * v[2]))
    half = 0.5 * rho
    out = [None] * 27
    for i in range(13):
        along = None
        c = VEL[26 - i]
        for k in range(3):
            if c[k]:
                term = t[k]
                if along is None:
                    along = term if c[k] > 0 else -term
                else:
                    along = along + term if c[k] > 0 else along - term
        even = base + half * (along * along)
        odd = rho * along
        out[26 - i] = WEIGHT[i] * (even + odd)
        out[i] = WEIGHT[i] * (even - odd)
    out[13] = WEIGHT[13] * base
    return out


def kernel(
    pop_in, rates_in, frac_in, vel_in, dest_in, line_in,
    f_out, table_out, chosen_s, rank_s,
    rates, pop, frac, vel, dest, line,
    send_f, send_m, recv_f, recv_m, send_r, recv_r,
    keep, mix, post, edge_s, edge_r, z_s, z_r,
    match_s, cells,
    a_send, a_recv, h_send, h_recv,
):
    gz, gx = lax.axis_index("gz"), lax.axis_index("gx")
    me = gz * 32 + gx
    yy, zz, core = gx // 8, gx // 2 % 4, gx % 2
    at_x = [lax.rem(gz + a, 4) for a in range(4)]
    at_y = [lax.rem(yy + b, 4) * 8 for b in range(4)]
    at_z = [lax.rem(zz + c, 4) * 2 for c in range(4)]
    at_core = [core, 1 - core]

    def peer(o):
        return at_x[o[0]], at_y[o[1]] + (at_z[o[2]] + at_core[o[3]])

    barrier = pltpu.get_barrier_semaphore()
    for o in OFFSETS:
        pl.semaphore_signal(barrier, inc=1, device_id=peer(o), device_id_type=MESH)

    loads = [
        pltpu.make_async_copy(src, dst, sem)
        for src, dst, sem in (
            (dest_in, dest, h_send.at[0]),
            (line_in, line, h_send.at[1]),
            (vel_in, vel, h_send.at[2]),
            (frac_in, frac, a_send.at[1]),
            (pop_in, pop, h_send.at[3]),
            (rates_in, rates, h_send.at[4]),
        )
    ]
    for load in loads:
        load.start()

    earlier = one_hot(iota((GRAINS, GRAINS), 0) < iota((GRAINS, GRAINS), 1))
    loads[0].wait()
    target = dest[...]
    chosen = iota((DEV, GRAINS), 0) == target
    chosen_b = one_hot(chosen)
    chosen_s[...] = chosen_b
    before = nn(chosen_b, earlier)
    rank = jnp.sum(jnp.where(chosen, before, 0.0), axis=0, keepdims=True)
    rank_mask = jnp.where(iota((CAP, GRAINS), 0, F32) == rank, 1.0, 0.0)
    rank_s[...] = rank_mask

    loads[1].wait()
    loads[2].wait()
    speed = vel[...].astype(F32)
    values = [line[...].astype(F32)] + [speed[k : k + 1] for k in range(3)]
    rows = [rank_mask * v for v in values] + [jnp.zeros((DEV - 4 * CAP, GRAINS), F32)]
    send_m[...] = nt(chosen_b, jnp.concatenate(rows, axis=0).astype(BF16))

    loads[3].wait()
    place = target.astype(F32) * CAP + rank
    fractions = frac[...]
    for j in range(8):
        pick = one_hot(iota((128, GRAINS), 0, F32) + 128.0 * j == place)
        send_f[16 * j : 16 * j + 16] = nn(pick, fractions).astype(BF16).reshape(16, CAP, 128)
    recv_m[pl.ds(me, 1), :] = send_m[pl.ds(me, 1), :]
    recv_f[me] = send_f[me]

    pl.semaphore_wait(barrier, DEV - 1)

    def to_peer(o, src, dst, k, wide):
        d = peer(o)
        p = d[0] * 32 + d[1]
        pltpu.make_async_remote_copy(
            src_ref=src.at[p] if wide else src.at[pl.ds(p, 1)],
            dst_ref=dst.at[me] if wide else dst.at[pl.ds(me, 1)],
            send_sem=a_send.at[k],
            recv_sem=a_recv.at[k],
            device_id=d,
            device_id_type=MESH,
        ).start()

    def wait_all(src, dst, sem):
        pltpu.make_async_copy(src.at[pl.ds(0, DEV - 1)], dst.at[pl.ds(0, DEV - 1)], sem).wait()

    for k in range(DEV - 1 + LEAD):
        if k < DEV - 1:
            to_peer(OFFSETS[k], send_m, recv_m, 0, False)
        if k >= LEAD:
            to_peer(OFFSETS[k - LEAD], send_f, recv_f, 1, True)

    def collide(f, rho, mom, level):
        inverse = 1.0 / rho
        equil = equilibrium(rho, [m * inverse for m in mom])
        departure = [f[i] - equil[i] for i in range(27)]
        projected = along_axes(departure, to_moments)
        fluid = along_axes([projected[a] * (-rates[a]) for a in range(27)], from_moments)
        for i in range(27):
            keep[i, level] = f[i] + fluid[i]
            mix[i, level] = departure[26 - i] - f[i] - fluid[i]

    loads[4].wait()
    loads[5].wait()
    first = []
    for level in range(2):
        f = [pop[i, level] for i in range(27)]
        rho, mom = moments(f)
        first.append((rho, mom))
        collide(f, rho, mom, level)

    wait_all(send_m, recv_m, a_recv.at[0])
    diag = iota((CAP, 128), 0) == iota((CAP, 128), 1) % CAP
    spread = jnp.concatenate(
        [
            jnp.where(diag, jnp.broadcast_to(recv_m[s : s + 1, :], (CAP, 128)), 0.0)
            for s in range(DEV)
        ],
        axis=0,
    ).astype(BF16)
    sel = one_hot(iota((CAP, 128), 0) == iota((CAP, 128), 1) // CAP)
    info = nt(sel, spread)
    match = jnp.where(iota((16, SLOTS), 0, F32) == info[0:1], 1.0, 0.0)
    match_s[...] = match
    weights = jnp.concatenate(
        [match] + [match * info[k : k + 1] for k in range(1, 4)], axis=0
    ).astype(BF16)

    wait_all(send_f, recv_f, a_recv.at[1])
    summed = nn(weights, recv_f[...].reshape(SLOTS, 128))
    covers = []
    for level in range(2):
        at = lambda k: summed[16 * k + 8 * level : 16 * k + 8 * level + 8]
        solid = at(0)
        inverse = 1.0 / (1.0 + solid)
        covers.append((inverse, solid * inverse, [at(k) * inverse for k in range(1, 4)]))

    up, down = gz < 3, gz > 0
    right, left = lax.rem(gx + 1, 32), lax.rem(gx + 31, 32)
    sub = iota((8, 128), 0)

    def halo(step):
        def copy(k, src, dst, device):
            return pltpu.make_async_remote_copy(
                src_ref=src,
                dst_ref=dst,
                send_sem=h_send.at[k],
                recv_sem=h_recv.at[step, k],
                device_id=device,
                device_id_type=MESH,
            )

        def edge(k, side, row, rows, device):
            at = (step, side, slice(None), pl.ds(row, rows))
            return copy(k, edge_s.at[at], edge_r.at[at], device)

        return (
            [edge(0, 0, 0, 4, (gz, right)), edge(0, 1, 0, 4, (gz, left))],
            [edge(1, 0, 4, 1, (gz + 1, right)), edge(1, 1, 4, 1, (gz + 1, left))],
            [edge(2, 0, 5, 1, (gz - 1, right)), edge(2, 1, 5, 1, (gz - 1, left))],
            [copy(3, z_s.at[step, 0], z_r.at[step, 0], (gz + 1, gx))],
            [copy(4, z_s.at[step, 1], z_r.at[step, 1], (gz - 1, gx))],
        )

    def wait_bytes(step, k, sem):
        if k < 3:
            at = (step, slice(None), slice(None), pl.ds(*((0, 4), (4, 1), (5, 1))[k]))
            src, dst = edge_s.at[at], edge_r.at[at]
        else:
            src, dst = z_s.at[step, k - 3], z_r.at[step, k - 3]
        pltpu.make_async_copy(src, dst, sem).wait()

    sends = (None, up, down, up, down)
    comes = (None, down, up, down, up)

    def guarded(test, run):
        if test is None:
            run()
        else:
            pl.when(test)(run)

    def start(copies, groups):
        for k in groups:
            guarded(sends[k], lambda k=k: [c.start() for c in copies[k]] and None)

    def arrive(step, groups):
        for k in groups:
            guarded(comes[k], lambda k=k: wait_bytes(step, k, h_recv.at[step, k]))

    def sent(step):
        for k in range(5):
            guarded(sends[k], lambda k=k: wait_bytes(step, k, h_send.at[k]))

    def edge_row(i, origin):
        cz = VEL[i][0]
        if cz == 0:
            return origin
        if cz > 0:
            return 2 if origin == 0 else 4
        return 3 if origin == 1 else 5

    def shifted(value, i):
        _, cx, cy = VEL[i]
        if cx:
            value = pltpu.roll(value, cx % 8, 0)
            value = jnp.where(sub == (0 if cx > 0 else 7), 0.0, value)
        if cy:
            value = pltpu.roll(value, cy % 128, 1)
        return value

    def leave(step, rhos):
        copies = halo(step)
        equils = [equilibrium(rhos[level], covers[level][2]) for level in range(2)]

        def finish(i, level):
            value = keep[i, level] + covers[level][1] * (mix[i, level] + equils[level][i])
            post[i, level] = value
            return value

        for i in range(27):
            cx, cy = VEL[i][1:]
            if cx:
                for level in range(2):
                    value = finish(i, level)
                    side, row = (0, 7) if cx > 0 else (1, 0)
                    k = edge_row(i, level)
                    edge_s[step, side, cy + 1, k : k + 1, :] = value[row : row + 1]
        start(copies, (1, 2, 0))
        for i in range(27):
            if VEL[i][1] == 0:
                for level in range(2):
                    finish(i, level)
        for i in range(9):
            z_s[step, 0, i] = shifted(post[18 + i, 1], 18 + i)
            z_s[step, 1, i] = shifted(post[i, 0], i)
        start(copies, (3, 4))

    def inside(out):
        for i in range(27):
            for level in range(2):
                if 0 <= level - VEL[i][0] <= 1:
                    out[i, level] = shifted(post[i, level - VEL[i][0]], i)

    def through_walls(step, out):
        for i in range(9):
            out[18 + i, 0] = jnp.where(gz == 0, post[8 - i, 0], z_r[step, 0, i])
            out[i, 1] = jnp.where(gz == 3, post[26 - i, 1], z_r[step, 1, i])

    def moved_edges(step):
        return [
            [
                edge_r[step, side, cy + 1]
                if cy == 0
                else pltpu.roll(edge_r[step, side, cy + 1], cy % 128, 1)
                for cy in (-1, 0, 1)
            ]
            for side in range(2)
        ]

    def edge_values(edges, level):
        for i in range(27):
            cz, cx, cy = VEL[i]
            if cx:
                side = 0 if cx > 0 else 1
                origin = level - cz
                if origin < 0 or origin > 1:
                    k, wall = (4, gz == 0) if cz > 0 else (5, gz == 3)
                else:
                    k, wall = edge_row(i, origin), None
                row = edges[side][cy + 1][k : k + 1]
                yield i, (0 if cx > 0 else 7), row, wall

    leave(0, [first[level][0] for level in range(2)])
    inside(cells)
    partial = []
    for level in range(2):
        f = [
            cells[i, level] if 0 <= level - VEL[i][0] <= 1 else None for i in range(27)
        ]
        partial.append(moments(f))
    arrive(0, (3, 4))
    through_walls(0, cells)
    for level in range(2):
        f = [
            None if 0 <= level - VEL[i][0] <= 1 else cells[i, level] for i in range(27)
        ]
        partial[level] = add_moments(partial[level], moments(f))
    arrive(0, (0, 1, 2))
    edges = moved_edges(0)
    fixes = []
    for level in range(2):
        f = {0: [None] * 27, 7: [None] * 27}
        for i, x, row, wall in edge_values(edges, level):
            if wall is not None:
                row = jnp.where(wall, 0.0, row)
            f[x][i] = jnp.broadcast_to(row, (8, 128))
        for x in (0, 7):
            rho, mom = moments(f[x])
            here = sub == x
            extra = (jnp.where(here, rho, 0.0), [jnp.where(here, m, 0.0) for m in mom])
            partial[level] = add_moments(partial[level], extra)
    second = partial
    pushes = [[None, None] for _ in range(3)]
    for level in range(2):
        rho, mom = second[level]
        inverse, _, us = covers[level]
        rho_sum = first[level][0] + rho
        for k in range(3):
            pushes[k][level] = ((first[level][1][k] + mom[k]) - us[k] * rho_sum) * inverse


    push = jnp.concatenate([pushes[k][level] for k in range(3) for level in range(2)], axis=0)
    high, low = split(push)
    grains = recv_f[...].reshape(SLOTS, 128)
    all_lines = nt(high, grains) + nt(low, grains)
    match = match_s[...]
    diag = iota((CAP, SLOTS), 0) == iota((CAP, SLOTS), 1) % CAP
    parts = []
    for k in range(3):
        force = jnp.sum(match * all_lines[16 * k : 16 * k + 16], axis=0, keepdims=True)
        parts.append(jnp.where(diag, force, 0.0))
    halves = split(jnp.concatenate(parts, axis=0))
    owner = one_hot(iota((DEV, SLOTS), 0) == iota((DEV, SLOTS), 1) // CAP)
    both = jnp.concatenate([h.astype(F32) for h in halves] + [jnp.zeros((DEV - 48, SLOTS), F32)], axis=0)
    send_r[...] = nt(owner, both.astype(BF16))
    recv_r[pl.ds(me, 1), :] = send_r[pl.ds(me, 1), :]
    for o in OFFSETS:
        to_peer(o, send_r, recv_r, 2, False)

    for level in range(2):
        for i, x, row, wall in edge_values(edges, level):
            if wall is not None:
                row = jnp.where(wall, cells[i, level, x : x + 1, :], row)
            cells[i, level, x : x + 1, :] = row
    for level in range(2):
        f = [cells[i, level] for i in range(27)]
        rho, mom = second[level]
        collide(f, rho, mom, level)
    sent(0)
    leave(1, [second[level][0] for level in range(2)])
    inside(f_out)
    arrive(1, (3, 4))
    through_walls(1, f_out)
    arrive(1, (0, 1, 2))
    edges = moved_edges(1)
    for level in range(2):
        for i, x, row, wall in edge_values(edges, level):
            if wall is not None:
                row = jnp.where(wall, f_out[i, level, x : x + 1, :], row)
            f_out[i, level, x : x + 1, :] = row
    for i in range(27):
        for level in range(2):
            f_out[i, level] = f_out[i, level] * (1.0 / WEIGHT[i])

    wait_all(send_r, recv_r, a_recv.at[2])
    table_out[...] = recv_r[...]

    wait_all(send_m, recv_m, a_send.at[0])
    wait_all(send_f, recv_f, a_send.at[1])
    wait_all(send_r, recv_r, a_send.at[2])
    sent(1)


def write_out(cells, table_in, chosen_in, rank_in, cells_out, force_out, force, sem):
    first = pltpu.make_async_copy(cells, cells_out, sem.at[0])
    first.start()
    table = table_in[...].T[0 : 6 * CAP].astype(BF16)
    per_grain = nn(table, chosen_in[...])
    rank_mask = rank_in[...]
    for k in range(3):
        at = CAP * k
        total = per_grain[at : at + CAP] + per_grain[24 + at : 24 + at + CAP]
        force[k : k + 1, :] = jnp.sum(rank_mask * total, axis=0, keepdims=True)
    second = pltpu.make_async_copy(force, force_out, sem.at[1])
    second.start()
    first.wait()
    second.wait()


def per_device(populations, rates, grain_fraction, grain_velocity, grain_dest, grain_line):
    hbm = pl.BlockSpec(memory_space=pl.ANY)
    vmem = pl.BlockSpec(memory_space=pltpu.VMEM)
    dma = pltpu.SemaphoreType.DMA
    block = (27, 2, 8, 128)
    parts = pl.pallas_call(
        kernel,
        out_shape=(
            pltpu.VMEM(block, F32),
            pltpu.VMEM((DEV, 128), F32),
            pltpu.VMEM((DEV, GRAINS), BF16),
            pltpu.VMEM((CAP, GRAINS), F32),
        ),
        in_specs=[hbm] * 6,
        out_specs=(vmem,) * 4,
        scratch_shapes=[
            pltpu.SMEM((27,), F32),
            pltpu.VMEM(block, F32),
            pltpu.VMEM((GRAINS, 128), BF16),
            pltpu.VMEM((3, GRAINS), BF16),
            pltpu.VMEM((1, GRAINS), jnp.int32),
            pltpu.VMEM((1, GRAINS), jnp.int32),
            pltpu.VMEM((DEV, CAP, 128), BF16),
            pltpu.VMEM((DEV, 128), F32),
            pltpu.VMEM((DEV, CAP, 128), BF16),
            pltpu.VMEM((DEV, 128), F32),
            pltpu.VMEM((DEV, 128), F32),
            pltpu.VMEM((DEV, 128), F32),
            pltpu.VMEM(block, F32),
            pltpu.VMEM(block, F32),
            pltpu.VMEM(block, F32),
            pltpu.VMEM((2, 2, 3, 8, 128), F32),
            pltpu.VMEM((2, 2, 3, 8, 128), F32),
            pltpu.VMEM((2, 2, 9, 8, 128), F32),
            pltpu.VMEM((2, 2, 9, 8, 128), F32),
            pltpu.VMEM((16, SLOTS), F32),
            pltpu.VMEM(block, F32),
            dma((3,)),
            dma((3,)),
            dma((5,)),
            dma((2, 5)),
        ],
        compiler_params=pltpu.CompilerParams(collective_id=0, has_side_effects=True),
        name="lattice",
    )(
        populations,
        rates,
        grain_fraction,
        grain_velocity,
        grain_dest.reshape(1, GRAINS),
        grain_line.reshape(1, GRAINS),
    )
    return pl.pallas_call(
        write_out,
        out_shape=(jax.ShapeDtypeStruct(block, F32), jax.ShapeDtypeStruct((3, GRAINS), F32)),
        in_specs=[hbm, vmem, vmem, vmem],
        out_specs=(hbm, hbm),
        scratch_shapes=[pltpu.VMEM((3, GRAINS), F32), dma((2,))],
        compiler_params=pltpu.CompilerParams(vmem_limit_bytes=1 << 20),
        name="write_out",
    )(*parts)


def solution(mesh):
    in_specs = (
        P(None, "gz", "gx", None),
        P(),
        P(("gz", "gx"), None),
        P(None, ("gz", "gx")),
        P(("gz", "gx"), None),
        P(("gz", "gx")),
    )
    out_specs = (P(None, "gz", "gx", None), P(None, ("gz", "gx")))
    return jax.shard_map(
        per_device, mesh=mesh, in_specs=in_specs, out_specs=out_specs, check_vma=False
    )
```

```python
import functools
import itertools

import jax
import jax.numpy as jnp
from jax import lax
from jax.experimental import pallas as pl
from jax.experimental.pallas import tpu as pltpu
from jax.sharding import PartitionSpec as P

MESH = pl.DeviceIdType.MESH
F32 = jnp.float32
BF16 = jnp.bfloat16
DEV = 128
CAP = 8
GRAINS = 512
SLOTS = DEV * CAP
VEL = [(i // 9 - 1, i // 3 % 3 - 1, i % 3 - 1) for i in range(27)]
WEIGHT = [(8.0 / 27, 2.0 / 27, 1.0 / 54, 1.0 / 216)[sum(map(abs, c))] for c in VEL]
NT = (((1,), (1,)), ((), ()))


def ring(v):
    return min(v, 4 - v)


OFFSETS = sorted(
    (o for o in itertools.product(range(4), range(4), range(4), range(2)) if any(o)),
    key=lambda o: -(0.75 * (ring(o[0]) + ring(o[1]) + ring(o[2])) + 0.5 * sum(v > 0 for v in o[:3]) + 0.2 * o[3]),
)


LEAD = 32


def iota(shape, dim, dtype=jnp.int32):
    out = lax.broadcasted_iota(jnp.int32, shape, dim)
    return out if dtype == jnp.int32 else out.astype(dtype)


def one_hot(mask):
    return jnp.where(mask, 1.0, 0.0).astype(BF16)


def split(x):
    high = x.astype(BF16)
    low = (x - high.astype(F32)).astype(BF16)
    return high, low


def nt(a, b):
    return lax.dot_general(a, b, NT, preferred_element_type=F32)


def nn(a, b):
    return jnp.dot(a, b, preferred_element_type=F32)


def along_axes(values, triple):
    for stride in (1, 3, 9):
        out = [None] * 27
        for base in range(27):
            if base // stride % 3 == 0:
                idx = (base, base + stride, base + 2 * stride)
                for k, v in zip(idx, triple(*(values[j] for j in idx))):
                    out[k] = v
        values = out
    return values


def to_moments(a, b, c):
    s = a + c
    return s + b, c - a, s


def from_moments(m0, m1, m2):
    h0, h1 = 0.5 * m2, 0.5 * m1
    return h0 - h1, m0 - m2, h0 + h1


def moments(f):
    plane = {}
    for i in range(27):
        if f[i] is not None:
            for key in [None] + [(k, VEL[i][k]) for k in range(3) if VEL[i][k]]:
                plane[key] = f[i] if key not in plane else plane[key] + f[i]

    def along(k):
        if (k, 1) not in plane:
            return -plane[(k, -1)] if (k, -1) in plane else jnp.zeros_like(plane[None])
        return plane[(k, 1)] - plane[(k, -1)] if (k, -1) in plane else plane[(k, 1)]

    return plane[None], [along(k) for k in range(3)]


def add_moments(a, b):
    return a[0] + b[0], [p + q for p, q in zip(a[1], b[1])]


def equilibrium(rho, v):
    t = [3.0 * q for q in v]
    base = rho * (1.0 - 1.5 * (v[0] * v[0] + v[1] * v[1] + v[2] * v[2]))
    half = 0.5 * rho
    out = [None] * 27
    for i in range(13):
        along = None
        c = VEL[26 - i]
        for k in range(3):
            if c[k]:
                term = t[k]
                if along is None:
                    along = term if c[k] > 0 else -term
                else:
                    along = along + term if c[k] > 0 else along - term
        even = base + half * (along * along)
        odd = rho * along
        out[26 - i] = WEIGHT[i] * (even + odd)
        out[i] = WEIGHT[i] * (even - odd)
    out[13] = WEIGHT[13] * base
    return out


def kernel(
    pop_in, rates_in, frac_in, vel_in, dest_in, line_in,
    f_out, table_out, chosen_s, rank_s,
    rates, pop, frac, vel, dest, line,
    send_f, send_m, recv_f, recv_m, send_r, recv_r,
    keep, mix, post, edge_s, edge_r, z_s, z_r,
    match_s, cells,
    a_send, a_recv, h_send, h_recv,
):
    gz, gx = lax.axis_index("gz"), lax.axis_index("gx")
    me = gz * 32 + gx
    yy, zz, core = gx // 8, gx // 2 % 4, gx % 2
    at_x = [lax.rem(gz + a, 4) for a in range(4)]
    at_y = [lax.rem(yy + b, 4) * 8 for b in range(4)]
    at_z = [lax.rem(zz + c, 4) * 2 for c in range(4)]
    at_core = [core, 1 - core]

    def peer(o):
        return at_x[o[0]], at_y[o[1]] + (at_z[o[2]] + at_core[o[3]])

    barrier = pltpu.get_barrier_semaphore()
    for o in OFFSETS:
        pl.semaphore_signal(barrier, inc=1, device_id=peer(o), device_id_type=MESH)

    loads = [
        pltpu.make_async_copy(src, dst, sem)
        for src, dst, sem in (
            (dest_in, dest, h_send.at[0]),
            (line_in, line, h_send.at[1]),
            (vel_in, vel, h_send.at[2]),
            (frac_in, frac, a_send.at[1]),
            (pop_in, pop, h_send.at[3]),
            (rates_in, rates, h_send.at[4]),
        )
    ]
    for load in loads:
        load.start()

    earlier = one_hot(iota((GRAINS, GRAINS), 0) < iota((GRAINS, GRAINS), 1))
    loads[0].wait()
    target = dest[...]
    chosen = iota((DEV, GRAINS), 0) == target
    chosen_b = one_hot(chosen)
    chosen_s[...] = chosen_b
    before = nn(chosen_b, earlier)
    rank = jnp.sum(jnp.where(chosen, before, 0.0), axis=0, keepdims=True)
    rank_mask = jnp.where(iota((CAP, GRAINS), 0, F32) == rank, 1.0, 0.0)
    rank_s[...] = rank_mask

    loads[1].wait()
    loads[2].wait()
    speed = vel[...].astype(F32)
    values = [line[...].astype(F32)] + [speed[k : k + 1] for k in range(3)]
    rows = [rank_mask * v for v in values] + [jnp.zeros((DEV - 4 * CAP, GRAINS), F32)]
    send_m[...] = nt(chosen_b, jnp.concatenate(rows, axis=0).astype(BF16))

    loads[3].wait()
    place = target.astype(F32) * CAP + rank
    fractions = frac[...]
    for j in range(8):
        pick = one_hot(iota((128, GRAINS), 0, F32) + 128.0 * j == place)
        send_f[16 * j : 16 * j + 16] = nn(pick, fractions).astype(BF16).reshape(16, CAP, 128)
    recv_m[pl.ds(me, 1), :] = send_m[pl.ds(me, 1), :]
    recv_f[me] = send_f[me]

    pl.semaphore_wait(barrier, DEV - 1)

    def to_peer(o, src, dst, k, wide):
        d = peer(o)
        p = d[0] * 32 + d[1]
        pltpu.make_async_remote_copy(
            src_ref=src.at[p] if wide else src.at[pl.ds(p, 1)],
            dst_ref=dst.at[me] if wide else dst.at[pl.ds(me, 1)],
            send_sem=a_send.at[k],
            recv_sem=a_recv.at[k],
            device_id=d,
            device_id_type=MESH,
        ).start()

    def wait_all(src, dst, sem):
        pltpu.make_async_copy(src.at[pl.ds(0, DEV - 1)], dst.at[pl.ds(0, DEV - 1)], sem).wait()

    for k in range(DEV - 1 + LEAD):
        if k < DEV - 1:
            to_peer(OFFSETS[k], send_m, recv_m, 0, False)
        if k >= LEAD:
            to_peer(OFFSETS[k - LEAD], send_f, recv_f, 1, True)

    def collide(f, rho, mom, level):
        inverse = 1.0 / rho
        equil = equilibrium(rho, [m * inverse for m in mom])
        departure = [f[i] - equil[i] for i in range(27)]
        projected = along_axes(departure, to_moments)
        fluid = along_axes([projected[a] * (-rates[a]) for a in range(27)], from_moments)
        for i in range(27):
            keep[i, level] = f[i] + fluid[i]
            mix[i, level] = departure[26 - i] - f[i] - fluid[i]

    loads[4].wait()
    loads[5].wait()
    first = []
    for level in range(2):
        f = [pop[i, level] for i in range(27)]
        rho, mom = moments(f)
        first.append((rho, mom))
        collide(f, rho, mom, level)

    wait_all(send_m, recv_m, a_recv.at[0])
    diag = iota((CAP, 128), 0) == iota((CAP, 128), 1) % CAP
    spread = jnp.concatenate(
        [
            jnp.where(diag, jnp.broadcast_to(recv_m[s : s + 1, :], (CAP, 128)), 0.0)
            for s in range(DEV)
        ],
        axis=0,
    ).astype(BF16)
    sel = one_hot(iota((CAP, 128), 0) == iota((CAP, 128), 1) // CAP)
    info = nt(sel, spread)
    match = jnp.where(iota((16, SLOTS), 0, F32) == info[0:1], 1.0, 0.0)
    match_s[...] = match
    weights = jnp.concatenate(
        [match] + [match * info[k : k + 1] for k in range(1, 4)], axis=0
    ).astype(BF16)

    wait_all(send_f, recv_f, a_recv.at[1])
    summed = nn(weights, recv_f[...].reshape(SLOTS, 128))
    covers = []
    for level in range(2):
        at = lambda k: summed[16 * k + 8 * level : 16 * k + 8 * level + 8]
        solid = at(0)
        inverse = 1.0 / (1.0 + solid)
        covers.append((inverse, solid * inverse, [at(k) * inverse for k in range(1, 4)]))

    up, down = gz < 3, gz > 0
    right, left = lax.rem(gx + 1, 32), lax.rem(gx + 31, 32)
    sub = iota((8, 128), 0)

    def halo(step):
        def copy(k, src, dst, device):
            return pltpu.make_async_remote_copy(
                src_ref=src,
                dst_ref=dst,
                send_sem=h_send.at[k],
                recv_sem=h_recv.at[step, k],
                device_id=device,
                device_id_type=MESH,
            )

        def edge(k, side, row, rows, device):
            at = (step, side, slice(None), pl.ds(row, rows))
            return copy(k, edge_s.at[at], edge_r.at[at], device)

        return (
            [edge(0, 0, 0, 4, (gz, right)), edge(0, 1, 0, 4, (gz, left))],
            [edge(1, 0, 4, 1, (gz + 1, right)), edge(1, 1, 4, 1, (gz + 1, left))],
            [edge(2, 0, 5, 1, (gz - 1, right)), edge(2, 1, 5, 1, (gz - 1, left))],
            [copy(3, z_s.at[step, 0], z_r.at[step, 0], (gz + 1, gx))],
            [copy(4, z_s.at[step, 1], z_r.at[step, 1], (gz - 1, gx))],
        )

    def wait_bytes(step, k, sem):
        if k < 3:
            at = (step, slice(None), slice(None), pl.ds(*((0, 4), (4, 1), (5, 1))[k]))
            src, dst = edge_s.at[at], edge_r.at[at]
        else:
            src, dst = z_s.at[step, k - 3], z_r.at[step, k - 3]
        pltpu.make_async_copy(src, dst, sem).wait()

    sends = (None, up, down, up, down)
    comes = (None, down, up, down, up)

    def guarded(test, run):
        if test is None:
            run()
        else:
            pl.when(test)(run)

    def start(copies, groups):
        for k in groups:
            guarded(sends[k], lambda k=k: [c.start() for c in copies[k]] and None)

    def arrive(step, groups):
        for k in groups:
            guarded(comes[k], lambda k=k: wait_bytes(step, k, h_recv.at[step, k]))

    def sent(step):
        for k in range(5):
            guarded(sends[k], lambda k=k: wait_bytes(step, k, h_send.at[k]))

    def edge_row(i, origin):
        cz = VEL[i][0]
        if cz == 0:
            return origin
        if cz > 0:
            return 2 if origin == 0 else 4
        return 3 if origin == 1 else 5

    def shifted(value, i):
        _, cx, cy = VEL[i]
        if cx:
            value = pltpu.roll(value, cx % 8, 0)
            value = jnp.where(sub == (0 if cx > 0 else 7), 0.0, value)
        if cy:
            value = pltpu.roll(value, cy % 128, 1)
        return value

    def leave(step, rhos):
        copies = halo(step)
        equils = [equilibrium(rhos[level], covers[level][2]) for level in range(2)]

        def finish(i, level):
            value = keep[i, level] + covers[level][1] * (mix[i, level] + equils[level][i])
            post[i, level] = value
            return value

        for i in range(27):
            cx, cy = VEL[i][1:]
            if cx:
                for level in range(2):
                    value = finish(i, level)
                    side, row = (0, 7) if cx > 0 else (1, 0)
                    k = edge_row(i, level)
                    edge_s[step, side, cy + 1, k : k + 1, :] = value[row : row + 1]
        start(copies, (1, 2, 0))
        for i in range(27):
            if VEL[i][1] == 0:
                for level in range(2):
                    finish(i, level)
        for i in range(9):
            z_s[step, 0, i] = shifted(post[18 + i, 1], 18 + i)
            z_s[step, 1, i] = shifted(post[i, 0], i)
        start(copies, (3, 4))

    def inside(out):
        for i in range(27):
            for level in range(2):
                if 0 <= level - VEL[i][0] <= 1:
                    out[i, level] = shifted(post[i, level - VEL[i][0]], i)

    def through_walls(step, out):
        for i in range(9):
            out[18 + i, 0] = jnp.where(gz == 0, post[8 - i, 0], z_r[step, 0, i])
            out[i, 1] = jnp.where(gz == 3, post[26 - i, 1], z_r[step, 1, i])

    def moved_edges(step):
        return [
            [
                edge_r[step, side, cy + 1]
                if cy == 0
                else pltpu.roll(edge_r[step, side, cy + 1], cy % 128, 1)
                for cy in (-1, 0, 1)
            ]
            for side in range(2)
        ]

    def edge_values(edges, level):
        for i in range(27):
            cz, cx, cy = VEL[i]
            if cx:
                side = 0 if cx > 0 else 1
                origin = level - cz
                if origin < 0 or origin > 1:
                    k, wall = (4, gz == 0) if cz > 0 else (5, gz == 3)
                else:
                    k, wall = edge_row(i, origin), None
                row = edges[side][cy + 1][k : k + 1]
                yield i, (0 if cx > 0 else 7), row, wall

    leave(0, [first[level][0] for level in range(2)])
    inside(cells)
    partial = []
    for level in range(2):
        f = [
            cells[i, level] if 0 <= level - VEL[i][0] <= 1 else None for i in range(27)
        ]
        partial.append(moments(f))
    arrive(0, (3, 4))
    through_walls(0, cells)
    for level in range(2):
        f = [
            None if 0 <= level - VEL[i][0] <= 1 else cells[i, level] for i in range(27)
        ]
        partial[level] = add_moments(partial[level], moments(f))
    arrive(0, (0, 1, 2))
    edges = moved_edges(0)
    fixes = []
    for level in range(2):
        f = {0: [None] * 27, 7: [None] * 27}
        for i, x, row, wall in edge_values(edges, level):
            if wall is not None:
                row = jnp.where(wall, 0.0, row)
            f[x][i] = jnp.broadcast_to(row, (8, 128))
        for x in (0, 7):
            rho, mom = moments(f[x])
            here = sub == x
            extra = (jnp.where(here, rho, 0.0), [jnp.where(here, m, 0.0) for m in mom])
            partial[level] = add_moments(partial[level], extra)
    second = partial
    pushes = [[None, None] for _ in range(3)]
    for level in range(2):
        rho, mom = second[level]
        inverse, _, us = covers[level]
        rho_sum = first[level][0] + rho
        for k in range(3):
            pushes[k][level] = ((first[level][1][k] + mom[k]) - us[k] * rho_sum) * inverse


    push = jnp.concatenate([pushes[k][level] for k in range(3) for level in range(2)], axis=0)
    high, low = split(push)
    grains = recv_f[...].reshape(SLOTS, 128)
    all_lines = nt(high, grains) + nt(low, grains)
    match = match_s[...]
    diag = iota((CAP, SLOTS), 0) == iota((CAP, SLOTS), 1) % CAP
    parts = []
    for k in range(3):
        force = jnp.sum(match * all_lines[16 * k : 16 * k + 16], axis=0, keepdims=True)
        parts.append(jnp.where(diag, force, 0.0))
    halves = split(jnp.concatenate(parts, axis=0))
    owner = one_hot(iota((DEV, SLOTS), 0) == iota((DEV, SLOTS), 1) // CAP)
    both = jnp.concatenate([h.astype(F32) for h in halves] + [jnp.zeros((DEV - 48, SLOTS), F32)], axis=0)
    send_r[...] = nt(owner, both.astype(BF16))
    recv_r[pl.ds(me, 1), :] = send_r[pl.ds(me, 1), :]
    for o in OFFSETS:
        to_peer(o, send_r, recv_r, 2, False)

    for level in range(2):
        for i, x, row, wall in edge_values(edges, level):
            if wall is not None:
                row = jnp.where(wall, cells[i, level, x : x + 1, :], row)
            cells[i, level, x : x + 1, :] = row
    for level in range(2):
        f = [cells[i, level] for i in range(27)]
        rho, mom = second[level]
        collide(f, rho, mom, level)
    sent(0)
    leave(1, [second[level][0] for level in range(2)])
    inside(f_out)
    arrive(1, (3, 4))
    through_walls(1, f_out)
    arrive(1, (0, 1, 2))
    edges = moved_edges(1)
    for level in range(2):
        for i, x, row, wall in edge_values(edges, level):
            if wall is not None:
                row = jnp.where(wall, f_out[i, level, x : x + 1, :], row)
            f_out[i, level, x : x + 1, :] = row
    for i in range(27):
        for level in range(2):
            f_out[i, level] = f_out[i, level] * (1.0 / WEIGHT[i])

    wait_all(send_m, recv_m, a_send.at[0])
    wait_all(send_f, recv_f, a_send.at[1])
    sent(1)
    wait_all(send_r, recv_r, a_send.at[2])
    wait_all(send_r, recv_r, a_recv.at[2])
    table_out[...] = recv_r[...]


def write_out(cells, table_in, chosen_in, rank_in, cells_out, force_out, force, sem):
    first = pltpu.make_async_copy(cells, cells_out, sem.at[0])
    first.start()
    table = table_in[...].T[0 : 6 * CAP].astype(BF16)
    per_grain = nn(table, chosen_in[...])
    rank_mask = rank_in[...]
    for k in range(3):
        at = CAP * k
        total = per_grain[at : at + CAP] + per_grain[24 + at : 24 + at + CAP]
        force[k : k + 1, :] = jnp.sum(rank_mask * total, axis=0, keepdims=True)
    second = pltpu.make_async_copy(force, force_out, sem.at[1])
    second.start()
    first.wait()
    second.wait()


def per_device(populations, rates, grain_fraction, grain_velocity, grain_dest, grain_line):
    hbm = pl.BlockSpec(memory_space=pl.ANY)
    vmem = pl.BlockSpec(memory_space=pltpu.VMEM)
    dma = pltpu.SemaphoreType.DMA
    block = (27, 2, 8, 128)
    parts = pl.pallas_call(
        kernel,
        out_shape=(
            pltpu.VMEM(block, F32),
            pltpu.VMEM((DEV, 128), F32),
            pltpu.VMEM((DEV, GRAINS), BF16),
            pltpu.VMEM((CAP, GRAINS), F32),
        ),
        in_specs=[hbm] * 6,
        out_specs=(vmem,) * 4,
        scratch_shapes=[
            pltpu.SMEM((27,), F32),
            pltpu.VMEM(block, F32),
            pltpu.VMEM((GRAINS, 128), BF16),
            pltpu.VMEM((3, GRAINS), BF16),
            pltpu.VMEM((1, GRAINS), jnp.int32),
            pltpu.VMEM((1, GRAINS), jnp.int32),
            pltpu.VMEM((DEV, CAP, 128), BF16),
            pltpu.VMEM((DEV, 128), F32),
            pltpu.VMEM((DEV, CAP, 128), BF16),
            pltpu.VMEM((DEV, 128), F32),
            pltpu.VMEM((DEV, 128), F32),
            pltpu.VMEM((DEV, 128), F32),
            pltpu.VMEM(block, F32),
            pltpu.VMEM(block, F32),
            pltpu.VMEM(block, F32),
            pltpu.VMEM((2, 2, 3, 8, 128), F32),
            pltpu.VMEM((2, 2, 3, 8, 128), F32),
            pltpu.VMEM((2, 2, 9, 8, 128), F32),
            pltpu.VMEM((2, 2, 9, 8, 128), F32),
            pltpu.VMEM((16, SLOTS), F32),
            pltpu.VMEM(block, F32),
            dma((3,)),
            dma((3,)),
            dma((5,)),
            dma((2, 5)),
        ],
        compiler_params=pltpu.CompilerParams(collective_id=0, has_side_effects=True),
        name="lattice",
    )(
        populations,
        rates,
        grain_fraction,
        grain_velocity,
        grain_dest.reshape(1, GRAINS),
        grain_line.reshape(1, GRAINS),
    )
    return pl.pallas_call(
        write_out,
        out_shape=(jax.ShapeDtypeStruct(block, F32), jax.ShapeDtypeStruct((3, GRAINS), F32)),
        in_specs=[hbm, vmem, vmem, vmem],
        out_specs=(hbm, hbm),
        scratch_shapes=[pltpu.VMEM((3, GRAINS), F32), dma((2,))],
        compiler_params=pltpu.CompilerParams(vmem_limit_bytes=1 << 20),
        name="write_out",
    )(*parts)


def solution(mesh):
    in_specs = (
        P(None, "gz", "gx", None),
        P(),
        P(("gz", "gx"), None),
        P(None, ("gz", "gx")),
        P(("gz", "gx"), None),
        P(("gz", "gx")),
    )
    out_specs = (P(None, "gz", "gx", None), P(None, ("gz", "gx")))
    return jax.shard_map(
        per_device, mesh=mesh, in_specs=in_specs, out_specs=out_specs, check_vma=False
    )
```
